32 devices in a mesh: tm: 8 (over z, y), lat: 4 (over x, core).
Axes of the slice: x: 2, y: 2, z: 4, core: 2. Of those that a mesh axis runs over, the one named last changes fastest.
Arguments:
- traj: float32 [8, 83, 24, 192], P('tm', None, 'lat'), may hold values from -6 to 6
- noise: float32 [8, 83, 24, 192], P('tm', None, 'lat'), may hold values from -6 to 6
- step_index: int32 [8], P('tm'), may hold values from 0 to 999
- embed_weight: bfloat16 [83, 512], replicated, may hold values from -0.625 to 0.625
- time_weight: float32 [512, 512], replicated, may hold values from -0.25 to 0.25
- dw_weight: float32 [512, 25], replicated, may hold values from -1.25 to 1.25
- ln_gain: float32 [512], replicated, may hold values from 0.5 to 1.5
- up_weight: bfloat16 [512, 1024], replicated, may hold values from -0.25 to 0.25
- down_weight: bfloat16 [1024, 512], replicated, may hold values from -0.1875 to 0.1875
- out_weight: bfloat16 [512, 83], replicated, may hold values from -0.25 to 0.25
Outputs:
- trajectory: float32 [8, 83, 24, 192], P('tm', None, 'lat')
The draws below stay inside these ranges and needn't reach their ends.
All inputs are finite; a program needn't handle non-finite values.
Results may differ from the reference program's by a relative error of at most 0.0025.
Values may be sent and summed in bfloat16 or wider, within the bound.
No kernel may reach another device: no remote copies, remote signals or barrier semaphores. Data moves between devices by JAX's collectives and lax.ppermute only.
A program may use at most 128 MiB of HBM per device.

```python
import math
import jax
import jax.numpy as jnp
from jax import lax

D = 512
FF = 1024
CH = 83
LON = 192
ITERS = 2
LEVELS = 1000
TIMES = 8
NLAT = 24


def place_ends(drawn, rng, least, high):
    longest = drawn.shape.index(max(drawn.shape))
    spots = []
    for shift in (0, 1):
        where = [jax.random.randint(jax.random.fold_in(rng, axis), (), 0, length) for axis, length in enumerate(drawn.shape)]
        where[longest] = (where[longest] + shift) % drawn.shape[longest]
        spots.append(tuple(where))
    return drawn.at[spots[0]].set(least).at[spots[1]].set(high)


def block_scale(own_key, dims, shards, smallest, high):
    level, own = 1.0, jax.random.fold_in(own_key, 6)
    for axis_at, shards_of in shards:
        draws = jnp.exp(jax.random.uniform(jax.random.fold_in(own, axis_at), (shards_of,), jnp.float32, smallest / len(shards), high / len(shards)))
        level = level * jnp.repeat(draws, dims[axis_at] // shards_of).reshape([-1 if axis == axis_at else 1 for axis in range(len(dims))])
    return level


def bell_draw(rng, dims, spread, most, cuts=(), held_as=jnp.bfloat16):
    values = spread * jax.random.normal(rng, dims, jnp.float32)
    if cuts:
        values = values * block_scale(rng, dims, cuts, -0.22, 0.18)
    return jnp.clip(values, -most, most).astype(held_as)


def setup_inputs(seed: int = 0) -> dict:
    streams_of = jax.random.split(jax.random.key(seed), 11)
    return {
        "traj": bell_draw(streams_of[0], (TIMES, CH, NLAT, LON), 1.0, 6.0, ((0, 8), (2, 4)), jnp.float32),
        "noise": bell_draw(streams_of[1], (TIMES, CH, NLAT, LON), 1.0, 6.0, ((0, 8), (2, 4)), jnp.float32),
        "step_index": place_ends(jax.random.randint(streams_of[2], (TIMES,), 0, LEVELS), jax.random.fold_in(streams_of[2], 1), 0, LEVELS - 1).astype(jnp.int32),
        "embed_weight": bell_draw(streams_of[3], (CH, D), CH ** -0.5, 0.625),
        "time_weight": bell_draw(streams_of[4], (D, D), D ** -0.5, 0.25, (), jnp.float32),
        "dw_weight": bell_draw(streams_of[5], (D, 25), 25 ** -0.5, 1.25, (), jnp.float32),
        "ln_gain": jnp.clip(1.0 + 0.1 * jax.random.normal(streams_of[6], (D,), jnp.float32), 0.5, 1.5),
        "up_weight": bell_draw(streams_of[7], (D, FF), D ** -0.5, 0.25),
        "down_weight": bell_draw(streams_of[8], (FF, D), FF ** -0.5, 0.1875),
        "out_weight": bell_draw(streams_of[9], (D, CH), D ** -0.5, 0.25),
    }


def noise_levels(step_index):
    log_ratio = math.log(0.1) / (LEVELS - 1)
    return 2.0 * jnp.exp(step_index.astype(jnp.float32) * log_ratio)

def conditions(noise_level, time_weight):
    half_width = time_weight.shape[0] // 2
    frequency = jnp.exp(jnp.arange(half_width, dtype=jnp.float32) * (-math.log(100.0) / half_width))
    angles = jnp.log(noise_level)[:, None] * frequency[None, :]
    features = jnp.concatenate([jnp.cos(angles), jnp.sin(angles)], axis=1)
    return jax.nn.silu(jnp.dot(features, time_weight, precision=lax.Precision.HIGHEST))

def depthwise_taps(lat_padded, dw_weight):
    lat_rows = lat_padded.shape[1] - 4
    widened = lat_padded.astype(jnp.float32)
    lon_cols = widened.shape[2]
    widened = jnp.concatenate([widened[:, :, -2:], widened, widened[:, :, :2]], axis=2)
    summed = jnp.zeros((widened.shape[0], lat_rows, lon_cols), jnp.float32)
    for row_tap in range(5):
        for col_tap in range(5):
            summed = summed + dw_weight[:, row_tap * 5 + col_tap][:, None, None] * widened[:, row_tap:row_tap + lat_rows, col_tap:col_tap + lon_cols]
    return summed

def denoise(current, condition, embed_weight, dw_weight, ln_gain, up_weight, down_weight, out_weight):
    channels, lat_rows, lon_cols = current.shape
    as_rows = current.astype(jnp.bfloat16).reshape(channels, lat_rows * lon_cols)
    embedded = jnp.dot(embed_weight.T, as_rows, preferred_element_type=jnp.float32)
    activation = (embedded + condition[:, None]).astype(jnp.bfloat16)
    width = activation.shape[0]
    padded = jnp.pad(activation.reshape(width, lat_rows, lon_cols), ((0, 0), (2, 2), (0, 0)))
    convolved = depthwise_taps(padded, dw_weight).reshape(width, lat_rows * lon_cols)
    average = lax.optimization_barrier(jnp.mean(convolved, axis=0))
    centred = convolved - average[None, :]
    variance = lax.optimization_barrier(jnp.mean(centred * centred, axis=0))
    normed = (centred * lax.rsqrt(variance + 1e-06)[None, :] * ln_gain[:, None]).astype(jnp.bfloat16)
    hidden = jax.nn.gelu(jnp.dot(up_weight.T, normed, preferred_element_type=jnp.float32), approximate=True).astype(jnp.bfloat16)
    block_out = (activation.astype(jnp.float32) + jnp.dot(down_weight.T, hidden, preferred_element_type=jnp.float32)).astype(jnp.bfloat16)
    return jnp.dot(out_weight.T, block_out, preferred_element_type=jnp.float32).reshape(channels, lat_rows, lon_cols)

def reference(traj, noise, step_index, embed_weight, time_weight, dw_weight, ln_gain, up_weight, down_weight, out_weight):
    noise_level = noise_levels(step_index)
    condition = conditions(noise_level, time_weight)
    root = traj[0]
    current = traj
    for picard_step in range(ITERS):

        def one_time(pieces):
            state_now, cond_now, level_now, noise_now = pieces
            drift_term = denoise(state_now, cond_now, embed_weight, dw_weight, ln_gain, up_weight, down_weight, out_weight)
            return 0.125 * level_now * drift_term + 0.125 * jnp.sqrt(level_now) * noise_now
        increment = lax.map(one_time, (current, condition, noise_level, noise))
        earlier = jnp.cumsum(increment, axis=0) - increment
        current = root[None] + earlier
    return current
```

```python
import functools
import math

import jax
import jax.numpy as jnp
from jax import lax
from jax.experimental import pallas as pl
from jax.experimental.pallas import tpu as pltpu
from jax.sharding import PartitionSpec as P

ITERS = 2
LEVELS = 1000
LANES = 128
LEAD = 8


def noise_levels(step_index):
    log_ratio = math.log(0.1) / (LEVELS - 1)
    return 2.0 * jnp.exp(step_index.astype(jnp.float32) * log_ratio)


def conditions(noise_level, time_weight):
    half_width = time_weight.shape[0] // 2
    frequency = jnp.exp(jnp.arange(half_width, dtype=jnp.float32) * (-math.log(100.0) / half_width))
    angles = jnp.log(noise_level)[:, None] * frequency[None, :]
    features = jnp.concatenate([jnp.cos(angles), jnp.sin(angles)], axis=1)
    return jax.nn.silu(jnp.dot(features, time_weight, precision=lax.Precision.HIGHEST))


def denoise_kernel(
    sizes, scal_ref, flag_ref, *refs
):
    pieces, half, lon, chunks = sizes
    states = refs[:pieces]
    (cond_ref, emb_ref, dw_ref, gain_ref, up_ref, down_ref, out_ref,
     g0_ref, g1_ref, inc0_ref, inc1_ref, act_ref, conv_ref, bo_ref) = refs[pieces:]
    h = flag_ref[0]
    edge = flag_ref[1]
    width = chunks * LANES

    emb = emb_ref[...]
    for slot in range(2):
        cond = cond_ref[slot : slot + 1, :]
        for kind, ref in (("own", states[slot]), ("outer", states[2 + slot])):
            rows = ref.shape[1] // lon
            if kind == "own":
                base = 2 * (1 - h)
                scale = None
            else:
                base = 5 * h
                scale = edge.astype(jnp.float32)
            turned = ref[...].T
            for r in range(rows):
                z = jnp.dot(turned[r * lon : (r + 1) * lon, :], emb, preferred_element_type=jnp.float32)
                a = (z + cond).astype(jnp.bfloat16).astype(jnp.float32)
                if scale is not None:
                    a = a * scale
                for c in range(chunks):
                    piece = a[:, c * LANES : (c + 1) * LANES]
                    act_ref[slot, c, base + r, LEAD : LEAD + lon, :] = piece
                    act_ref[slot, c, base + r, 0:LEAD, :] = piece[lon - LEAD : lon, :]
                    act_ref[slot, c, base + r, LEAD + lon : 2 * LEAD + lon, :] = piece[0:LEAD, :]

    def conv_chunk(i, carry):
        slot = i // chunks
        c = i % chunks
        taps = [jnp.broadcast_to(dw_ref[c, k : k + 1, :], (8, LANES)) for k in range(25)]

        def conv_block(b, carry):
            col = pl.multiple_of(b * 8, 8)
            sums = [None] * half
            for rr in range(half + 4):
                for j in range(5):
                    x = act_ref[slot, c, rr, pl.ds(col + LEAD - 2 + j, 8), :]
                    for o in range(half):
                        k = rr - o
                        if 0 <= k < 5:
                            t = taps[k * 5 + j] * x
                            sums[o] = t if sums[o] is None else sums[o] + t
            for o in range(half):
                conv_ref[slot, o, c, pl.ds(col, 8), :] = sums[o]
            return carry

        return lax.fori_loop(0, lon // 8, conv_block, carry)

    lax.fori_loop(0, 2 * chunks, conv_chunk, 0)

    def mix(i, carry):
        slot = i // half
        o = i % half
        x = [conv_ref[slot, o, c] for c in range(chunks)]
        mean = sum(jnp.sum(v, axis=1, keepdims=True) for v in x) * (1.0 / width)
        x = [v - mean for v in x]
        var = sum(jnp.sum(v * v, axis=1, keepdims=True) for v in x) * (1.0 / width)
        inv = lax.rsqrt(var + 1e-06)
        n = jnp.concatenate(
            [(v * inv * gain_ref[:, c * LANES : (c + 1) * LANES]).astype(jnp.bfloat16) for c, v in enumerate(x)], axis=1
        )
        u = jnp.dot(n, up_ref[...], preferred_element_type=jnp.float32)
        hid = jax.nn.gelu(u, approximate=True).astype(jnp.bfloat16)
        d = jnp.dot(hid, down_ref[...], preferred_element_type=jnp.float32)
        a = jnp.concatenate([act_ref[slot, c, 2 + o, LEAD : LEAD + lon, :] for c in range(chunks)], axis=1)
        bo_ref[slot, pl.ds(pl.multiple_of(o * lon, 16), lon), :] = (a + d).astype(jnp.bfloat16)
        return carry

    lax.fori_loop(0, 2 * half, mix, 0)

    for slot, (g_ref, inc_ref) in enumerate(((g0_ref, inc0_ref), (g1_ref, inc1_ref))):
        drift = lax.dot_general(
            out_ref[...], bo_ref[slot], (((1,), (1,)), ((), ())), preferred_element_type=jnp.float32
        )
        inc_ref[...] = scal_ref[slot] * drift + g_ref[...]


def denoise(states, cond, coef, flags, weights, g_own, g_part, half, lon):
    channels = g_own.shape[0]
    width = cond.shape[1]
    chunks = width // LANES
    emb, dw, gain, up, down, out = weights
    vmem = pl.BlockSpec(memory_space=pltpu.VMEM)
    smem = pl.BlockSpec(memory_space=pltpu.SMEM)
    points = half * lon
    shape = jax.ShapeDtypeStruct((channels, points), jnp.float32)
    flops = 2 * 2 * points * width * (channels * 2 + 2 * up.shape[1] + 25)
    return pl.pallas_call(
        functools.partial(denoise_kernel, (len(states), half, lon, chunks)),
        out_shape=(shape, shape),
        in_specs=[smem, smem] + [vmem] * (len(states) + 9),
        out_specs=(vmem, vmem),
        scratch_shapes=[
            pltpu.VMEM((2, chunks, half + 4, lon + 2 * LEAD, LANES), jnp.float32),
            pltpu.VMEM((2, half, chunks, lon, LANES), jnp.float32),
            pltpu.VMEM((2, points, width), jnp.bfloat16),
        ],
        cost_estimate=pl.CostEstimate(flops=flops, bytes_accessed=4 << 20, transcendentals=2 * points * up.shape[1]),
        compiler_params=pltpu.CompilerParams(vmem_limit_bytes=48 << 20),
    )(coef, flags, *states, cond, emb, dw, gain, up, down, out, g_own, g_part)


def pair_sums(total, groups, swap, memory):
    earlier = None
    kept = []
    unit = 1
    stage = 0
    cur = total
    while unit < groups:
        before = memory[stage] if memory else None
        sent = (cur - before[0] if before else cur).astype(jnp.bfloat16)
        known = sent.astype(jnp.float32) + (before[0] if before else 0.0)
        got = before[1] if before else jnp.zeros_like(total)
        for step in (3, 2, 1):
            if step * unit < groups:
                shift = 2 * step * unit
                perm = [(i, i + shift) for i in range(2 * groups - shift)]
                got = got + lax.ppermute(sent, "tm", perm).astype(jnp.float32)
        kept.append((known, got))
        earlier = got if earlier is None else earlier + got
        cur = cur + got
        unit *= 4
        stage += 1
    return earlier, kept


def shards(
    traj, noise, step_index, embed_weight, time_weight, dw_weight, ln_gain, up_weight, down_weight, out_weight,
):
    times, bands = lax.axis_size("tm"), lax.axis_size("lat")
    t, l = lax.axis_index("tm"), lax.axis_index("lat")
    y = t % 2
    h = (y + l) % 2
    first = t // 2 == 0
    groups = times // 2
    channels, rows, lon = traj.shape[1:]
    half = rows // 2
    width = embed_weight.shape[1]
    both = ("tm", "lat")

    def at(a, b):
        return a * bands + b

    cells = [(a, b, (a + b) % 2) for a in range(times) for b in range(bands)]
    swap = [(at(a, b), at(a ^ 1, b)) for a, b, _ in cells]
    side = [(at(a, b), at(a, b + (1 if c else -1))) for a, b, c in cells if 0 <= b + (1 if c else -1) < bands]
    cross = [(at(a, b), at(a ^ 1, b + (-1 if c else 1))) for a, b, c in cells if 0 <= b + (-1 if c else 1) < bands]

    def cut(x, start, count):
        return lax.dynamic_slice_in_dim(x, start, count, axis=1).reshape(channels, count * lon)

    root = traj[0]
    v = root.astype(jnp.bfloat16)
    part5 = lax.ppermute(cut(v, 1 - h, half + 2), both, swap)
    own_out = lax.ppermute(cut(v, (rows - 2) * h, 2), both, side)
    part_out = lax.ppermute(cut(v, (rows - 2) * (1 - h), 2), both, cross)
    own5 = cut(v, h, half + 2)
    index2 = jnp.concatenate([step_index, lax.ppermute(step_index, both, swap)])

    level = noise_levels(step_index)[0]
    fixed = 0.125 * jnp.sqrt(level) * noise[0] + jnp.where(t == 0, root, 0.0)
    g_own = cut(fixed, half * h, half)
    g_part = lax.ppermute(cut(fixed, half * (1 - h), half), both, swap)

    levels2 = noise_levels(index2)
    cond = conditions(levels2, time_weight)
    coef = 0.125 * levels2
    edge = jnp.where(jnp.where(h == 0, l > 0, l < bands - 1), 1, 0)
    flags = jnp.stack([h, edge]).astype(jnp.int32)
    chunks = width // LANES
    dw = dw_weight.T.reshape(25, chunks, LANES).transpose(1, 0, 2)
    weights = (embed_weight, dw, ln_gain.reshape(1, width), up_weight, down_weight, out_weight.T)

    states = (own5, part5, own_out, part_out)
    memory = None
    for picard_step in range(ITERS):
        inc_own, inc_part = denoise(states, cond, coef, flags, weights, g_own, g_part, half, lon)
        earlier, memory = pair_sums(inc_own + inc_part, groups, swap, memory)
        inc_even = jnp.where(y == 0, inc_own, inc_part)
        now_own = earlier + jnp.where(y == 1, inc_even, 0.0)
        now_part = earlier + jnp.where(y == 0, inc_even, 0.0)
        if picard_step + 1 < ITERS:
            start_own = cut(v, half * h, half)
            start_part = jnp.where(h == 0, part5[:, : half * lon], part5[:, 2 * lon :])
            s_own = jnp.where(first & (y == 0), start_own, now_own.astype(jnp.bfloat16))
            s_part = jnp.where(first & (y == 1), start_part, now_part.astype(jnp.bfloat16))
            s = jnp.stack([s_own, s_part])
            low, high = s[:, :, : 2 * lon], s[:, :, (half - 2) * lon :]
            inner = lax.ppermute(jnp.where(h == 0, high, low), both, swap)
            outer = lax.ppermute(jnp.where(h == 0, low, high), both, side)
            inner = inner[::-1]
            s5 = jnp.where(
                h == 0, jnp.concatenate([s, inner], axis=2), jnp.concatenate([inner, s], axis=2)
            )
            states = (s5[0], s5[1], outer[0], outer[1])
    other = lax.ppermute(now_part, both, swap)
    mine = now_own
    upper = jnp.where(h == 0, mine, other).reshape(channels, half, lon)
    lower = jnp.where(h == 0, other, mine).reshape(channels, half, lon)
    result = jnp.concatenate([upper, lower], axis=1)
    return jnp.where(t == 0, root, result)[None]


def solution(mesh):
    in_specs = (P("tm", None, "lat", None), P("tm", None, "lat", None), P("tm")) + (P(),) * 7
    out_specs = P("tm", None, "lat", None)
    return jax.shard_map(shards, mesh=mesh, in_specs=in_specs, out_specs=out_specs, check_vma=False)
```

```python
import functools
import math

import jax
import jax.numpy as jnp
from jax import lax
from jax.experimental import pallas as pl
from jax.experimental.pallas import tpu as pltpu
from jax.sharding import PartitionSpec as P

ITERS = 2
LEVELS = 1000
LANES = 128
LEAD = 8
RADIX = 4
BF16 = jnp.bfloat16
F32 = jnp.float32
VMEM = pl.BlockSpec(memory_space=pltpu.VMEM)
SMEM = pl.BlockSpec(memory_space=pltpu.SMEM)
ANY = pl.BlockSpec(memory_space=pl.ANY)
LIMIT = pltpu.CompilerParams(vmem_limit_bytes=48 << 20)


def place():
    t, l = lax.axis_index("tm"), lax.axis_index("lat")
    return t, l, t % 2, (t + l) % 2


def level_of(index):
    return 2.0 * jnp.exp(index * (math.log(0.1) / (LEVELS - 1)))


def prep_kernel(idx_ref, traj_ref, own_ref, swap_ref, side_ref, cross_ref, v_ref):
    channels, rows, _, lon = traj_ref.shape
    half = rows // 2
    _, _, _, h = place()
    for r in range(rows):
        v_ref[:, r * lon : (r + 1) * lon] = traj_ref[:, r, 0, :].astype(BF16)
    span, near = (half + 2) * lon, 2 * lon

    def cut(upper):
        low, high = v_ref[:, :span], v_ref[:, lon : lon + span]
        first, last = v_ref[:, :near], v_ref[:, (rows - 2) * lon :]
        own_ref[...] = low if upper else high
        swap_ref[:channels, :] = high if upper else low
        side_ref[...] = first if upper else last
        cross_ref[...] = last if upper else first

    @pl.when(h == 0)
    def _():
        cut(True)

    @pl.when(h == 1)
    def _():
        cut(False)

    index = idx_ref[0]
    swap_ref[channels : channels + 1, :] = jnp.full((1, span), index // 32, F32).astype(BF16)
    swap_ref[channels + 1 : channels + 2, :] = jnp.full((1, span), index % 32, F32).astype(BF16)


def noise_kernel(idx_ref, traj_ref, noise_ref, own_ref, send_ref):
    channels, rows, _, lon = traj_ref.shape
    half = rows // 2
    t, _, _, h = place()
    scale = 0.125 * jnp.sqrt(level_of(jnp.full((1, lon), idx_ref[0], F32)))
    anchor = jnp.where(t == 0, 1.0, 0.0)
    for r in range(rows):
        value = scale * noise_ref[:, r, 0, :] + anchor * traj_ref[:, r, 0, :]
        here = h == r // half
        cols = slice((r % half) * lon, (r % half + 1) * lon)

        @pl.when(here)
        def _():
            own_ref[:, cols] = value

        @pl.when(jnp.logical_not(here))
        def _():
            send_ref[:, cols] = value


def denoise_kernel(first, sizes, *refs):
    half, lon, chunks, ff = sizes
    width = chunks * LANES
    channels = None
    refs = list(refs)

    def take(n):
        got = refs[:n]
        del refs[:n]
        return got

    (idx_ref,) = take(1)
    if first:
        own5, part5, outer_own, outer_part = take(4)
        (time_hbm,) = take(1)
    else:
        s_own, s_part, inner, outer = take(4)
        cond_in, coef_in, sent_in = take(3)
    hbm = take(8)
    sent_ref, even_ref, total_ref = take(3)
    if first:
        cond_ref, coef_ref = take(2)
    else:
        cond_ref, coef_ref = cond_in, coef_in
    bufs = take(8)
    if first:
        (time_buf,) = take(1)
    act_ref, conv_ref, norm_ref, hid_ref, bo_ref, sems = take(6)
    emb_ref, dw_ref, gain_ref, up_ref, down_ref, out_ref, g0_ref, g1_ref = bufs

    t, l, y, h = place()
    bands = lax.axis_size("lat")
    copies = [pltpu.make_async_copy(s, d, sems.at[i]) for i, (s, d) in enumerate(zip(hbm, bufs))]
    if first:
        copies.append(pltpu.make_async_copy(time_hbm, time_buf, sems.at[8]))
        copies[8].start()
    for c in copies[:8]:
        c.start()
    emb_c, dw_c, gain_c, up_c, down_c, out_c, g0_c, g1_c = copies[:8]

    if first:
        quarter = width // 2
        mine = jnp.full((1, quarter), idx_ref[0], F32)
        rows = part5.shape[0]
        theirs = part5[83:84, :quarter].astype(F32) * 32.0 + part5[84:85, :quarter].astype(F32)
        index = jnp.concatenate([mine, theirs, jnp.zeros((6, quarter), F32)], axis=0)
        level = level_of(index)
        coef_ref[...] = 0.125 * level[:, :LANES]
        step = lax.broadcasted_iota(jnp.int32, (8, quarter), 1).astype(F32)
        angle = jnp.log(level) * jnp.exp(step * (-math.log(100.0) / quarter))
        features = jnp.concatenate([jnp.cos(angle), jnp.sin(angle)], axis=1)
        copies[8].wait()
        z = jnp.dot(features, time_buf[...], precision=lax.Precision.HIGHEST, preferred_element_type=F32)
        cond_ref[...] = z / (1.0 + jnp.exp(-z))

    emb_c.wait()
    emb = emb_ref[...]
    channels = emb.shape[0]
    border = jnp.where(jnp.where(h == 0, l > 0, l < bands - 1), 1.0, 0.0)
    inside = 5 * (1 - h)
    outside = 5 * h
    for slot in range(2):
        cond = cond_ref[slot : slot + 1, :]
        if first:
            pieces = (
                ((own5, part5)[slot][:channels, :], 2 * (1 - h), None),
                ((outer_own, outer_part)[slot][...], outside, border),
            )
        else:
            near = 2 * lon
            back = slice((1 - slot) * near, (2 - slot) * near)
            pieces = (
                ((s_own, s_part)[slot][...], 2, None),
                (inner[:, back], inside, None),
                (outer[:, slot * near : (slot + 1) * near], outside, border),
            )
        for value, base, scale in pieces:
            turned = value.T
            for r in range(value.shape[1] // lon):
                z = jnp.dot(turned[r * lon : (r + 1) * lon, :], emb, preferred_element_type=F32)
                a = (z + cond).astype(BF16).astype(F32)
                if scale is not None:
                    a = a * scale
                for c in range(chunks):
                    piece = a[:, c * LANES : (c + 1) * LANES]
                    act_ref[slot, c, base + r, LEAD : LEAD + lon, :] = piece
                    act_ref[slot, c, base + r, 0:LEAD, :] = piece[lon - LEAD : lon, :]
                    act_ref[slot, c, base + r, LEAD + lon : 2 * LEAD + lon, :] = piece[0:LEAD, :]

    part = lon // 2

    def conv(i):
        slot, o, flip = i // half, i % half, i % 2
        for c in range(chunks):
            for p in range(2):
                total = None
                for rr in range(5):
                    for j in range(5):
                        x = act_ref[slot, c, o + rr, LEAD - 2 + j + p * part : LEAD - 2 + j + (p + 1) * part, :]
                        x = x * dw_ref[rr * 5 + j : rr * 5 + j + 1, c * LANES : (c + 1) * LANES]
                        total = x if total is None else total + x
                conv_ref[c, p * part : (p + 1) * part, :] = total
        for p in range(2):
            x = [conv_ref[c, p * part : (p + 1) * part, :] for c in range(chunks)]
            mean = jnp.sum(functools.reduce(jnp.add, x), axis=1, keepdims=True) * (1.0 / width)
            x = [v - mean for v in x]
            var = jnp.sum(functools.reduce(jnp.add, [v * v for v in x]), axis=1, keepdims=True) * (1.0 / width)
            inv = lax.rsqrt(var + 1e-06)
            for c, v in enumerate(x):
                lane = slice(c * LANES, (c + 1) * LANES)
                norm_ref[flip, p * part : (p + 1) * part, lane] = (v * inv * gain_ref[:, lane]).astype(BF16)

    def mix(i):
        slot, o, flip = i // half, i % half, i % 2
        n = norm_ref[flip]
        k0 = math.sqrt(2.0 / math.pi)
        for b in range(0, ff, 256):
            u = jnp.dot(n, up_ref[:, b : b + 256], preferred_element_type=F32)
            hid_ref[:, b : b + 256] = (u + u * jnp.tanh(u * (k0 + (k0 * 0.044715) * (u * u)))).astype(BF16)
        for b in range(0, width, 256):
            d = jnp.dot(hid_ref[...], down_ref[:, b : b + 256], preferred_element_type=F32)
            for k in range(2):
                a = act_ref[slot, b // LANES + k, 2 + o, LEAD : LEAD + lon, :]
                lane = slice(b + k * LANES, b + (k + 1) * LANES)
                value = (a + 0.5 * d[:, k * LANES : (k + 1) * LANES]).astype(BF16)
                bo_ref[slot, pl.ds(pl.multiple_of(o * lon, 16), lon), lane] = value

    dw_c.wait()
    gain_c.wait()
    conv(0)
    up_c.wait()
    down_c.wait()

    def both(i, carry):
        conv(i)
        mix(i - 1)
        return carry

    lax.fori_loop(1, 2 * half, both, 0)
    mix(2 * half - 1)

    out_c.wait()
    g0_c.wait()
    g1_c.wait()
    incs = []
    for slot, g_ref in enumerate((g0_ref, g1_ref)):
        drift = lax.dot_general(out_ref[...], bo_ref[slot], (((1,), (1,)), ((), ())), preferred_element_type=F32)
        inc = coef_ref[slot : slot + 1, 0:1] * drift + g_ref[...]
        incs.append(inc)

        @pl.when(y == slot)
        def _():
            even_ref[...] = inc

    total = incs[0] + incs[1]
    if not first:
        total = total - sent_in[...].astype(F32)
    total_ref[...] = total
    sent_ref[...] = total.astype(BF16)


def denoise(first, head, weights, half, lon):
    emb, dw, gain, up, down, out, g_own, g_part = weights
    channels, points = g_own.shape
    width, ff = up.shape
    chunks = width // LANES
    grid = jax.ShapeDtypeStruct((channels, points), F32)
    outs = [jax.ShapeDtypeStruct((channels, points), BF16), grid, grid]
    if first:
        outs += [jax.ShapeDtypeStruct((8, width), F32), jax.ShapeDtypeStruct((8, LANES), F32)]
        specs = [SMEM] + [VMEM] * 4 + [ANY]
    else:
        specs = [SMEM] + [VMEM] * 7
    scratch = [pltpu.VMEM(w.shape, w.dtype) for w in weights]
    if first:
        scratch.append(pltpu.VMEM(head[-1].shape, F32))
    scratch += [
        pltpu.VMEM((2, chunks, half + 4, lon + 2 * LEAD, LANES), F32),
        pltpu.VMEM((chunks, lon, LANES), F32),
        pltpu.VMEM((2, lon, width), BF16),
        pltpu.VMEM((lon, ff), BF16),
        pltpu.VMEM((2, points, width), BF16),
        pltpu.SemaphoreType.DMA((9,)),
    ]
    flops = 2 * 2 * points * width * (channels * 2 + 2 * ff + 25)
    return pl.pallas_call(
        functools.partial(denoise_kernel, first, (half, lon, chunks, ff)),
        out_shape=tuple(outs),
        in_specs=specs + [ANY] * 8,
        out_specs=tuple([VMEM] * len(outs)),
        scratch_shapes=scratch,
        cost_estimate=pl.CostEstimate(flops=flops, bytes_accessed=4 << 20, transcendentals=2 * points * ff),
        compiler_params=LIMIT,
        name="denoise_first" if first else "denoise_later",
    )(*head, *weights)


def middle_kernel(count, lon, *refs):
    gots, refs = refs[:count], refs[count:]
    even, own5, part5, sum_ref, own_ref, part_ref, inner_ref, outer_ref = refs
    channels, points = even.shape
    t, _, y, h = place()
    near = 2 * lon
    total = gots[0][...].astype(F32)
    for g in gots[1:]:
        total = total + g[...].astype(F32)
    sum_ref[...] = total
    odd = (total + even[...]).astype(BF16)
    flat = total.astype(BF16)

    def emit(parity, upper):
        shift = 0 if upper else near
        start = (own5 if parity == 0 else part5)[:channels, shift : shift + points]
        state = jnp.where(t < 2, start.astype(F32), flat.astype(F32)).astype(BF16)
        pair = (state, odd) if parity == 0 else (odd, state)
        own_ref[...] = pair[0]
        part_ref[...] = pair[1]
        for k, s in enumerate(pair):
            cols = slice(k * near, (k + 1) * near)
            low, high = s[:, :near], s[:, points - near :]
            inner_ref[:, cols] = high if upper else low
            outer_ref[:, cols] = low if upper else high

    for parity in range(2):
        for half_at in range(2):

            @pl.when((y == parity) & (h == half_at))
            def _():
                emit(parity, half_at == 0)


def ending_kernel(count, *refs):
    gots, (before, even, mine_ref, send_ref) = refs[:count], refs[count:]
    _, _, y, _ = place()
    total = before[...]
    for g in gots:
        total = total + g[...].astype(F32)
    odd = total + even[...]
    mine_ref[...] = jnp.where(y == 0, total, odd)
    send_ref[...] = jnp.where(y == 0, odd, total)


def output_kernel(mine, other, traj_ref, out_ref):
    channels, rows, _, lon = out_ref.shape
    half = rows // 2
    t, _, _, h = place()
    for r in range(rows):
        cols = slice((r % half) * lon, (r % half + 1) * lon)
        value = jnp.where(h == r // half, mine[:, cols], other[:, cols])
        out_ref[:, r, 0, :] = jnp.where(t == 0, traj_ref[:, r, 0, :], value)


def call(body, outs, ins, specs=None, scratch=(), name=None):
    return pl.pallas_call(
        body,
        out_shape=tuple(jax.ShapeDtypeStruct(s, d) for s, d in outs),
        in_specs=specs or [VMEM] * len(ins),
        out_specs=tuple([VMEM] * len(outs)),
        scratch_shapes=list(scratch),
        compiler_params=LIMIT,
        name=name,
    )(*ins)


def exchange(sent, total, groups, memory):
    gots, kept = [], []
    base, moved, unit = sent, None, 1
    while unit < groups:
        if unit > 1:
            rest = memory[len(kept)] if memory else 0.0
            sent = (total + moved + rest).astype(BF16)
            kept.append(base.astype(F32) + moved + rest - sent.astype(F32))
        for step in range(RADIX - 1, 0, -1):
            shift = 2 * step * unit
            if shift < 2 * groups:
                gots.append(lax.ppermute(sent, "tm", [(i, i + shift) for i in range(2 * groups - shift)]))
        unit *= RADIX
        if groups > RADIX:
            moved = functools.reduce(jnp.add, [g.astype(F32) for g in gots])
    return gots, kept


def shards(
    traj, noise, step_index, embed_weight, time_weight, dw_weight, ln_gain, up_weight, down_weight, out_weight,
):
    times, bands = lax.axis_size("tm"), lax.axis_size("lat")
    groups = times // 2
    channels, rows, lon = traj.shape[1:]
    half = rows // 2
    width = embed_weight.shape[1]
    points, span, near = half * lon, (half + 2) * lon, 2 * lon
    axes = ("tm", "lat")

    def at(a, b):
        return a * bands + b

    cells = [(a, b, (a + b) % 2) for a in range(times) for b in range(bands)]
    swap = [(at(a, b), at(a ^ 1, b)) for a, b, _ in cells]
    side = [(at(a, b), at(a, b + (1 if c else -1))) for a, b, c in cells if 0 <= b + (1 if c else -1) < bands]
    cross = [(at(a, b), at(a ^ 1, b + (-1 if c else 1))) for a, b, c in cells if 0 <= b + (-1 if c else 1) < bands]

    root = traj.reshape(channels, rows, 1, lon)
    draws = noise.reshape(channels, rows, 1, lon)
    own5, to_swap, to_side, to_cross = call(
        prep_kernel,
        [((channels, span), BF16), ((88, span), BF16), ((channels, near), BF16), ((channels, near), BF16)],
        (step_index, root),
        [SMEM, VMEM],
        [pltpu.VMEM((channels, rows * lon), BF16)],
        "prep",
    )
    part5 = lax.ppermute(to_swap, axes, swap)
    outer_part = lax.ppermute(to_cross, axes, cross)
    outer_own = lax.ppermute(to_side, axes, side)
    g_own, g_send = call(
        noise_kernel, [((channels, points), F32)] * 2, (step_index, root, draws), [SMEM, VMEM, VMEM], name="noise"
    )
    g_part = lax.ppermute(g_send, axes, swap)
    weights = (
        embed_weight, dw_weight.T, ln_gain.reshape(1, width), up_weight, down_weight, out_weight.T, g_own, g_part,
    )

    sent, even, total, cond, coef = denoise(
        True, (step_index, own5, part5, outer_own, outer_part, time_weight), weights, half, lon
    )
    gots, memory = exchange(sent, total, groups, None)
    before = None
    for picard_step in range(1, ITERS):
        before, s_own, s_part, inner, outer = call(
            functools.partial(middle_kernel, len(gots), lon),
            [((channels, points), F32)] + [((channels, points), BF16)] * 2 + [((channels, 2 * near), BF16)] * 2,
            (*gots, even, own5, part5),
            name="middle",
        )
        inner = lax.ppermute(inner, axes, swap)
        outer = lax.ppermute(outer, axes, side)
        known = sent
        sent, even, total = denoise(False, (step_index, s_own, s_part, inner, outer, cond, coef, known), weights, half, lon)
        gots, memory = exchange(sent, total, groups, memory)
    mine, send = call(
        functools.partial(ending_kernel, len(gots)),
        [((channels, points), F32)] * 2,
        (*gots, before, even),
        name="ending",
    )
    other = lax.ppermute(send, axes, swap)
    (result,) = call(output_kernel, [((channels, rows, 1, lon), F32)], (mine, other, root), name="output")
    return result.reshape(1, channels, rows, lon)


def solution(mesh):
    in_specs = (P("tm", None, "lat", None), P("tm", None, "lat", None), P("tm")) + (P(),) * 7
    out_specs = P("tm", None, "lat", None)
    return jax.shard_map(shards, mesh=mesh, in_specs=in_specs, out_specs=out_specs, check_vma=False)
```

```python
import functools
import math

import jax
import jax.numpy as jnp
from jax import lax
from jax.experimental import pallas as pl
from jax.experimental.pallas import tpu as pltpu
from jax.sharding import PartitionSpec as P

ITERS = 2
LEVELS = 1000
LANES = 128
LEAD = 8
RADIX = 4
BF16 = jnp.bfloat16
F32 = jnp.float32
VMEM = pl.BlockSpec(memory_space=pltpu.VMEM)
SMEM = pl.BlockSpec(memory_space=pltpu.SMEM)
HBM = pl.BlockSpec(memory_space=pltpu.HBM)
VMEM_OR_HBM = pl.BlockSpec(memory_space=pl.ANY)
PAD = 88
LIMIT = pltpu.CompilerParams(vmem_limit_bytes=48 << 20)


def place():
    t, l = lax.axis_index("tm"), lax.axis_index("lat")
    return t, l, t % 2, (t + l) % 2


def level_of(index):
    return 2.0 * jnp.exp(index * (math.log(0.1) / (LEVELS - 1)))


def prep_kernel(idx_ref, traj_hbm, own_ref, swap_ref, side_ref, cross_ref, traj_ref, v_ref, sem):
    channels, rows, _, lon = traj_ref.shape
    half = rows // 2
    _, _, _, h = place()
    copy = pltpu.make_async_copy(traj_hbm, traj_ref, sem)
    copy.start()
    v_ref[channels:, :] = jnp.ones((PAD - channels, rows * lon), BF16)
    copy.wait()
    for r in range(rows):
        v_ref[:channels, r * lon : (r + 1) * lon] = traj_ref[:, r, 0, :].astype(BF16)
    span, near = (half + 2) * lon, 2 * lon

    def cut(upper):
        low, high = v_ref[:, :span], v_ref[:, lon : lon + span]
        first, last = v_ref[:, :near], v_ref[:, (rows - 2) * lon :]
        own_ref[...] = low if upper else high
        swap_ref[...] = high if upper else low
        side_ref[...] = first if upper else last
        cross_ref[...] = last if upper else first

    @pl.when(h == 0)
    def _():
        cut(True)

    @pl.when(h == 1)
    def _():
        cut(False)

    index = idx_ref[0]
    swap_ref[PAD - 2 : PAD - 1, :] = jnp.full((1, span), index // 32, F32).astype(BF16)
    swap_ref[PAD - 1 : PAD, :] = jnp.full((1, span), index % 32, F32).astype(BF16)


def noise_kernel(idx_ref, after_ref, traj_hbm, noise_hbm, own_ref, send_ref, traj_ref, noise_ref, sems):
    channels, rows, _, lon = traj_ref.shape
    half = rows // 2
    t, _, _, h = place()
    copy = pltpu.make_async_copy(noise_hbm, noise_ref, sems.at[0])
    copy.start()
    scale = 0.125 * jnp.sqrt(level_of(jnp.full((1, lon), idx_ref[0], F32)))

    def emit(upper, anchored):
        for r in range(rows):
            value = scale * noise_ref[:, r, 0, :]
            if anchored:
                value = value + traj_ref[:, r, 0, :]
            cols = slice((r % half) * lon, (r % half + 1) * lon)
            target = own_ref if (r < half) == upper else send_ref
            target[:, cols] = value

    @pl.when(t == 0)
    def _():
        root = pltpu.make_async_copy(traj_hbm, traj_ref, sems.at[1])
        root.start()
        root.wait()

    copy.wait()
    for upper in (True, False):
        for anchored in (True, False):

            @pl.when((h == (0 if upper else 1)) & ((t == 0) == anchored))
            def _():
                emit(upper, anchored)


def spread_out(main, extra):
    done = 0
    for i, unit in enumerate(main):
        unit()
        while done < len(extra) and done * len(main) < (i + 1) * len(extra):
            extra[done]()
            done += 1
    for unit in extra[done:]:
        unit()


def denoise_kernel(first, sizes, *refs):
    half, lon, chunks, ff, channels = sizes
    width = chunks * LANES
    refs = list(refs)

    def take(n):
        got = refs[:n]
        del refs[:n]
        return got

    (idx_ref,) = take(1)
    if first:
        own5, part5, outer_own, outer_part = take(4)
        (time_hbm,) = take(1)
    else:
        s_own, s_part, inner, outer = take(4)
        emb_in, coef_ref, sent_in = take(3)
    hbm = take(8)
    sent_ref, even_ref, total_ref = take(3)
    if first:
        emb_all, coef_ref = take(2)
    else:
        emb_all = emb_in
    bufs = take(8)
    if first:
        (time_buf,) = take(1)
    act_ref, conv_ref, norm_ref, up_out, hid_ref, bo_ref, sems = take(7)
    emb_ref, dw_ref, gain_ref, up_ref, down_ref, out_ref, g0_ref, g1_ref = bufs

    t, l, y, h = place()
    copies = [pltpu.make_async_copy(s, d, sems.at[i]) for i, (s, d) in enumerate(zip(hbm, bufs))]
    emb_c, dw_c, gain_c, up_c, down_c, out_c, g0_c, g1_c = copies
    if first:
        time_c = pltpu.make_async_copy(time_hbm, time_buf, sems.at[8])
        time_c.start()
    for c in copies:
        c.start()

    if first:
        quarter = width // 2
        mine = jnp.full((1, quarter), idx_ref[0], F32)
        theirs = part5[PAD - 2 : PAD - 1, :quarter].astype(F32) * 32.0 + part5[PAD - 1 : PAD, :quarter].astype(F32)
        index = jnp.concatenate([mine, theirs, jnp.zeros((6, quarter), F32)], axis=0)
        level = level_of(index)
        coef_ref[...] = 0.125 * level[:, :LANES]
        step = lax.broadcasted_iota(jnp.int32, (8, quarter), 1).astype(F32)
        angle = jnp.log(level) * jnp.exp(step * (-math.log(100.0) / quarter))
        features = jnp.concatenate([jnp.cos(angle), jnp.sin(angle)], axis=1)
        time_c.wait()
        z = jnp.dot(features, time_buf[...], precision=lax.Precision.HIGHEST, preferred_element_type=F32)
        cond = z / (1.0 + jnp.exp(-z))
        emb_c.wait()
        for slot in range(2):
            emb_all[slot, :channels, :] = emb_ref[...]
            emb_all[slot, channels:, :] = jnp.zeros((PAD - channels, width), BF16)
            rest = cond[slot : slot + 1, :]
            for k in range(3):
                piece = rest.astype(BF16)
                emb_all[slot, channels + k : channels + k + 1, :] = piece
                rest = rest - piece.astype(F32)
    else:
        emb_c.wait()

    inside = 5 * (1 - h)
    outside = 5 * h

    def embed_units(slot):
        units = []
        if first:
            pieces = (((own5, part5)[slot], None, 2 * (1 - h)), ((outer_own, outer_part)[slot], None, outside))
        else:
            near = 2 * lon
            pieces = (
                ((s_own, s_part)[slot], None, 2),
                (inner, slice((1 - slot) * near, (2 - slot) * near), inside),
                (outer, slice(slot * near, (slot + 1) * near), outside),
            )
        for ref, cols, base in pieces:
            count = (ref.shape[1] if cols is None else cols.stop - cols.start) // lon
            held = []

            def unit(r, ref=ref, cols=cols, base=base, held=held):
                if not held:
                    held.append((ref[...] if cols is None else ref[:, cols]).T)
                rows = held[0][r * lon : (r + 1) * lon, :]
                a = jnp.dot(rows, emb_all[slot], preferred_element_type=F32).astype(BF16).astype(F32)
                for c in range(chunks):
                    piece = a[:, c * LANES : (c + 1) * LANES]
                    act_ref[slot, c, base + r, LEAD : LEAD + lon, :] = piece
                    act_ref[slot, c, base + r, 0:LEAD, :] = piece[lon - LEAD : lon, :]
                    act_ref[slot, c, base + r, LEAD + lon : 2 * LEAD + lon, :] = piece[0:LEAD, :]

            units += [functools.partial(unit, r) for r in range(count)]
        return units

    part = lon // 2
    tile = 24

    def conv_units(b):
        slot, p = b // 2, b % 2
        flip = b % 2

        def tile_unit(c, k):
            col = p * part + k * tile
            taps = [dw_ref[q : q + 1, c * LANES : (c + 1) * LANES] for q in range(25)]
            sums = [None] * half
            for rr in range(half + 4):
                for j in range(5):
                    at = LEAD - 2 + j + col
                    x = act_ref[slot, c, rr, at : at + tile, :]
                    for o in range(half):
                        if 0 <= rr - o < 5:
                            v = x * taps[(rr - o) * 5 + j]
                            sums[o] = v if sums[o] is None else sums[o] + v
            for o in range(half):
                conv_ref[flip, c, o, k * tile : (k + 1) * tile, :] = sums[o]

        def norm_unit(o, k):
            span = slice(k * 48, (k + 1) * 48)
            x = [conv_ref[flip, c, o, span, :] for c in range(chunks)]
            mean = jnp.sum(functools.reduce(jnp.add, x), axis=1, keepdims=True) * (1.0 / width)
            x = [v - mean for v in x]
            var = jnp.sum(functools.reduce(jnp.add, [v * v for v in x]), axis=1, keepdims=True) * (1.0 / width)
            inv = lax.rsqrt(var + 1e-06)
            for c, v in enumerate(x):
                lane = slice(c * LANES, (c + 1) * LANES)
                value = (v * inv * gain_ref[:, lane]).astype(BF16)
                norm_ref[flip, o * part + k * 48 : o * part + (k + 1) * 48, lane] = value

        return [functools.partial(tile_unit, c, k) for c in range(chunks) for k in range(part // tile)] + [
            functools.partial(norm_unit, o, k) for o in range(half) for k in range(part // 48)
        ]

    k0 = math.sqrt(2.0 / math.pi)

    def mix_units(b):
        slot, p = b // 2, b % 2
        flip = b % 2
        count = half * part

        def up_unit(n):
            up_out[n % 2] = jnp.dot(norm_ref[flip], up_ref[:, n * 256 : (n + 1) * 256], preferred_element_type=F32)

        def gelu_unit(n, o):
            u = up_out[n % 2, o * part : (o + 1) * part, :]
            value = (u + u * jnp.tanh(u * (k0 + (k0 * 0.044715) * (u * u)))).astype(BF16)
            hid_ref[flip, o * part : (o + 1) * part, n * 256 : (n + 1) * 256] = value

        def down_unit(m):
            d = jnp.dot(hid_ref[flip], down_ref[:, m * 256 : (m + 1) * 256], preferred_element_type=F32)
            for o in range(half):
                for k in range(2):
                    c = 2 * m + k
                    a = act_ref[slot, c, 2 + o, LEAD + p * part : LEAD + (p + 1) * part, :]
                    value = (a + 0.5 * d[o * part : (o + 1) * part, k * LANES : (k + 1) * LANES]).astype(BF16)
                    start = o * lon + p * part
                    bo_ref[slot, start : start + part, c * LANES : (c + 1) * LANES] = value

        steps = ff // 256
        units = [functools.partial(up_unit, 0)]
        for n in range(steps):
            if n + 1 < steps:
                units.append(functools.partial(up_unit, n + 1))
            units += [functools.partial(gelu_unit, n, o) for o in range(half)]
        return units + [functools.partial(down_unit, m) for m in range(width // 256)]

    incs = []

    def out_unit(slot):
        drift = lax.dot_general(out_ref[...], bo_ref[slot], (((1,), (1,)), ((), ())), preferred_element_type=F32)
        incs.append(coef_ref[slot : slot + 1, 0:1] * drift + (g0_ref, g1_ref)[slot][...])

    for unit in embed_units(0):
        unit()
    dw_c.wait()
    gain_c.wait()
    spread_out(conv_units(0), embed_units(1))
    up_c.wait()
    down_c.wait()
    spread_out(conv_units(1), mix_units(0))
    spread_out(conv_units(2), mix_units(1))
    out_c.wait()
    g0_c.wait()
    g1_c.wait()
    spread_out(conv_units(3), mix_units(2) + [functools.partial(out_unit, 0)])
    for unit in mix_units(3):
        unit()
    out_unit(1)

    for slot in range(2):

        @pl.when(y == slot)
        def _():
            even_ref[...] = incs[slot]

    total = incs[0] + incs[1]
    if not first:
        total = total - sent_in[...].astype(F32)
    total_ref[...] = total
    sent_ref[...] = total.astype(BF16)


def denoise(first, head, weights, half, lon):
    emb, dw, gain, up, down, out, g_own, g_part = weights
    channels, points = g_own.shape
    width, ff = up.shape
    chunks = width // LANES
    grid = jax.ShapeDtypeStruct((channels, points), F32)
    outs = [jax.ShapeDtypeStruct((channels, points), BF16), grid, grid]
    if first:
        outs += [jax.ShapeDtypeStruct((2, PAD, width), BF16), jax.ShapeDtypeStruct((8, LANES), F32)]
        specs = [SMEM] + [VMEM] * 4 + [HBM]
    else:
        specs = [SMEM] + [VMEM] * 7
    scratch = [pltpu.VMEM(w.shape, w.dtype) for w in weights]
    if first:
        scratch.append(pltpu.VMEM(head[-1].shape, F32))
    block = points // 2
    scratch += [
        pltpu.VMEM((2, chunks, half + 4, lon + 2 * LEAD, LANES), F32),
        pltpu.VMEM((2, chunks, half, lon // 2, LANES), F32),
        pltpu.VMEM((2, block, width), BF16),
        pltpu.VMEM((2, block, 256), F32),
        pltpu.VMEM((2, block, ff), BF16),
        pltpu.VMEM((2, points, width), BF16),
        pltpu.SemaphoreType.DMA((9,)),
    ]
    flops = 2 * 2 * points * width * (channels * 2 + 2 * ff + 25)
    return pl.pallas_call(
        functools.partial(denoise_kernel, first, (half, lon, chunks, ff, channels)),
        out_shape=tuple(outs),
        in_specs=specs + [HBM] * 6 + [VMEM_OR_HBM] * 2,
        out_specs=tuple([VMEM] * len(outs)),
        scratch_shapes=scratch,
        cost_estimate=pl.CostEstimate(flops=flops, bytes_accessed=4 << 20, transcendentals=2 * points * ff),
        compiler_params=LIMIT,
        name="denoise_first" if first else "denoise_later",
    )(*head, *weights)


def middle_kernel(count, lon, *refs):
    gots, refs = refs[:count], refs[count:]
    even, own5, part5, sum_ref, own_ref, part_ref, inner_ref, outer_ref = refs
    channels, points = even.shape
    t, _, y, h = place()
    near = 2 * lon
    total = gots[0][...].astype(F32)
    for g in gots[1:]:
        total = total + g[...].astype(F32)
    sum_ref[...] = total
    odd = (total + even[...]).astype(BF16)
    flat = total.astype(BF16)
    for ref in (own_ref, part_ref, inner_ref, outer_ref):
        ref[channels:, :] = jnp.ones((PAD - channels, ref.shape[1]), BF16)

    def emit(parity, upper):
        shift = 0 if upper else near
        start = (own5 if parity == 0 else part5)[:channels, shift : shift + points]
        state = jnp.where(t < 2, start.astype(F32), flat.astype(F32)).astype(BF16)
        pair = (state, odd) if parity == 0 else (odd, state)
        own_ref[:channels, :] = pair[0]
        part_ref[:channels, :] = pair[1]
        for k, s in enumerate(pair):
            cols = slice(k * near, (k + 1) * near)
            low, high = s[:, :near], s[:, points - near :]
            inner_ref[:channels, cols] = high if upper else low
            outer_ref[:channels, cols] = low if upper else high

    for parity in range(2):
        for half_at in range(2):

            @pl.when((y == parity) & (h == half_at))
            def _():
                emit(parity, half_at == 0)


def ending_kernel(count, *refs):
    gots, (before, even, mine_ref, send_ref) = refs[:count], refs[count:]
    _, _, y, _ = place()
    total = before[...]
    for g in gots:
        total = total + g[...].astype(F32)
    odd = total + even[...]
    mine_ref[...] = jnp.where(y == 0, total, odd)
    send_ref[...] = jnp.where(y == 0, odd, total)


def output_kernel(mine, other, traj_hbm, out_ref, sem):
    channels, rows, _, lon = out_ref.shape
    half = rows // 2
    t, _, _, h = place()

    def emit(upper):
        for r in range(rows):
            cols = slice((r % half) * lon, (r % half + 1) * lon)
            out_ref[:, r, 0, :] = (mine if (r < half) == upper else other)[:, cols]

    @pl.when((h == 0) & (t > 0))
    def _():
        emit(True)

    @pl.when((h == 1) & (t > 0))
    def _():
        emit(False)

    @pl.when(t == 0)
    def _():
        copy = pltpu.make_async_copy(traj_hbm, out_ref, sem)
        copy.start()
        copy.wait()


def call(body, outs, ins, specs=None, scratch=(), name=None):
    return pl.pallas_call(
        body,
        out_shape=tuple(jax.ShapeDtypeStruct(s, d) for s, d in outs),
        in_specs=specs or [VMEM] * len(ins),
        out_specs=tuple([VMEM] * len(outs)),
        scratch_shapes=list(scratch),
        compiler_params=LIMIT,
        name=name,
    )(*ins)


def exchange(sent, total, groups, memory):
    gots, kept = [], []
    base, moved, unit = sent, None, 1
    while unit < groups:
        if unit > 1:
            rest = memory[len(kept)] if memory else 0.0
            sent = (total + moved + rest).astype(BF16)
            kept.append(base.astype(F32) + moved + rest - sent.astype(F32))
        for step in range(1, RADIX):
            shift = 2 * step * unit
            if shift < 2 * groups:
                gots.append(lax.ppermute(sent, "tm", [(i, i + shift) for i in range(2 * groups - shift)]))
        unit *= RADIX
        if groups > RADIX:
            moved = functools.reduce(jnp.add, [g.astype(F32) for g in gots])
    return gots, kept


def shards(
    traj, noise, step_index, embed_weight, time_weight, dw_weight, ln_gain, up_weight, down_weight, out_weight,
):
    times, bands = lax.axis_size("tm"), lax.axis_size("lat")
    groups = times // 2
    channels, rows, lon = traj.shape[1:]
    half = rows // 2
    width = embed_weight.shape[1]
    points, span, near = half * lon, (half + 2) * lon, 2 * lon
    axes = ("tm", "lat")

    def at(a, b):
        return a * bands + b

    cells = [(a, b, (a + b) % 2) for a in range(times) for b in range(bands)]
    swap = [(at(a, b), at(a ^ 1, b)) for a, b, _ in cells]
    side = [(at(a, b), at(a, b + (1 if c else -1))) for a, b, c in cells if 0 <= b + (1 if c else -1) < bands]
    cross = [(at(a, b), at(a ^ 1, b + (-1 if c else 1))) for a, b, c in cells if 0 <= b + (-1 if c else 1) < bands]

    root = traj.reshape(channels, rows, 1, lon)
    draws = noise.reshape(channels, rows, 1, lon)
    band = (channels, rows, 1, lon)
    own5, to_swap, to_side, to_cross = call(
        prep_kernel,
        [((PAD, span), BF16), ((PAD, span), BF16), ((PAD, near), BF16), ((PAD, near), BF16)],
        (step_index, root),
        [SMEM, HBM],
        [pltpu.VMEM(band, F32), pltpu.VMEM((PAD, rows * lon), BF16), pltpu.SemaphoreType.DMA],
        "prep",
    )
    part5 = lax.ppermute(to_swap, axes, swap)
    outer_part = lax.ppermute(to_cross, axes, cross)
    outer_own = lax.ppermute(to_side, axes, side)
    g_own, g_send = call(
        noise_kernel,
        [((channels, points), F32)] * 2,
        (step_index, own5, root, draws),
        [SMEM, VMEM, HBM, HBM],
        [pltpu.VMEM(band, F32), pltpu.VMEM(band, F32), pltpu.SemaphoreType.DMA((2,))],
        "noise",
    )
    g_part = lax.ppermute(g_send, axes, swap)
    weights = (
        embed_weight, dw_weight.T, ln_gain.reshape(1, width), up_weight, down_weight, out_weight.T, g_own, g_part,
    )

    sent, even, total, emb_all, coef = denoise(
        True, (step_index, own5, part5, outer_own, outer_part, time_weight), weights, half, lon
    )
    gots, memory = exchange(sent, total, groups, None)
    before = None
    for picard_step in range(1, ITERS):
        before, s_own, s_part, inner, outer = call(
            functools.partial(middle_kernel, len(gots), lon),
            [((channels, points), F32)] + [((PAD, points), BF16)] * 2 + [((PAD, 2 * near), BF16)] * 2,
            (*gots, even, own5, part5),
            name="middle",
        )
        inner = lax.ppermute(inner, axes, swap)
        outer = lax.ppermute(outer, axes, side)
        known = sent
        sent, even, total = denoise(False, (step_index, s_own, s_part, inner, outer, emb_all, coef, known), weights, half, lon)
        gots, memory = exchange(sent, total, groups, memory)
    mine, send = call(
        functools.partial(ending_kernel, len(gots)),
        [((channels, points), F32)] * 2,
        (*gots, before, even),
        name="ending",
    )
    other = lax.ppermute(send, axes, swap)
    (result,) = call(
        output_kernel, [(band, F32)], (mine, other, root), [VMEM, VMEM, HBM], [pltpu.SemaphoreType.DMA], "output"
    )
    return result.reshape(1, channels, rows, lon)


def solution(mesh):
    in_specs = (P("tm", None, "lat", None), P("tm", None, "lat", None), P("tm")) + (P(),) * 7
    out_specs = P("tm", None, "lat", None)
    return jax.shard_map(shards, mesh=mesh, in_specs=in_specs, out_specs=out_specs, check_vma=False)
```

```python
import functools
import math

import jax
import jax.numpy as jnp
from jax import lax
from jax.experimental import pallas as pl
from jax.experimental.pallas import tpu as pltpu
from jax.sharding import PartitionSpec as P


ITERS = 2
LEVELS = 1000
LANES = 128
LEAD = 8
RADIX = 4
TILE = 24
BF16 = jnp.bfloat16
F32 = jnp.float32
VMEM = pl.BlockSpec(memory_space=pltpu.VMEM)
SMEM = pl.BlockSpec(memory_space=pltpu.SMEM)
HBM = pl.BlockSpec(memory_space=pltpu.HBM)
VMEM_OR_HBM = pl.BlockSpec(memory_space=pl.ANY)
PAD = 88
LIMIT = pltpu.CompilerParams(vmem_limit_bytes=24 << 20)


def place():
    t, l = lax.axis_index("tm"), lax.axis_index("lat")
    return t, l, t % 2, (t + l) % 2


def level_of(index):
    return 2.0 * jnp.exp(index * (math.log(0.1) / (LEVELS - 1)))


def prep_kernel(idx_ref, traj_hbm, own_ref, inner_ref, swap_ref, side_ref, cross_ref, traj_ref, v_ref, sem):
    channels, rows, _, lon = traj_ref.shape
    half = rows // 2
    _, _, _, h = place()
    copy = pltpu.make_async_copy(traj_hbm, traj_ref, sem)
    copy.start()
    v_ref[channels:, :] = jnp.ones((PAD - channels, rows * lon), BF16)
    copy.wait()
    for r in range(rows):
        v_ref[:channels, r * lon : (r + 1) * lon] = traj_ref[:, r, 0, :].astype(BF16)
    span, near = (half + 2) * lon, 2 * lon

    def cut(upper):
        low, high = v_ref[:, :span], v_ref[:, lon : lon + span]
        first, last = v_ref[:, :near], v_ref[:, (rows - 2) * lon :]
        own_ref[...] = v_ref[:, : half * lon] if upper else v_ref[:, half * lon :]
        inner_ref[...] = v_ref[:, half * lon : span] if upper else v_ref[:, lon : half * lon]
        swap_ref[...] = high if upper else low
        side_ref[...] = first if upper else last
        cross_ref[...] = last if upper else first

    @pl.when(h == 0)
    def _():
        cut(True)

    @pl.when(h == 1)
    def _():
        cut(False)

    index = idx_ref[0]
    swap_ref[PAD - 2 : PAD - 1, :] = jnp.full((1, span), index // 32, F32).astype(BF16)
    swap_ref[PAD - 1 : PAD, :] = jnp.full((1, span), index % 32, F32).astype(BF16)


def condition_of(index, time_weight):
    half_width = index.shape[1]
    level = level_of(index)
    step = lax.broadcasted_iota(jnp.int32, index.shape, 1).astype(F32)
    angle = jnp.log(level) * jnp.exp(step * (-math.log(100.0) / half_width))
    features = jnp.concatenate([jnp.cos(angle), jnp.sin(angle)], axis=1)
    z = jnp.dot(features, time_weight, precision=lax.Precision.HIGHEST, preferred_element_type=F32)
    return z / (1.0 + jnp.exp(-z)), level


def fill_embedding(all_ref, emb, cond):
    channels, width = emb.shape
    all_ref[:channels, :] = emb
    all_ref[channels:, :] = jnp.zeros((PAD - channels, width), BF16)
    rest = cond
    for k in range(3):
        piece = rest.astype(BF16)
        all_ref[channels + k : channels + k + 1, :] = piece
        rest = rest - piece.astype(F32)


def embed_row(turned, r, lon, emb_all):
    return jnp.dot(turned[r * lon : (r + 1) * lon, :], emb_all, preferred_element_type=F32).astype(BF16)


def store_row(act_ref, row, a, lon):
    a = a.astype(F32)
    for c in range(a.shape[1] // LANES):
        piece = a[:, c * LANES : (c + 1) * LANES]
        act_ref[c, row, LEAD : LEAD + lon, :] = piece
        act_ref[c, row, 0:LEAD, :] = piece[lon - LEAD : lon, :]
        act_ref[c, row, LEAD + lon : 2 * LEAD + lon, :] = piece[0:LEAD, :]


def conv_tile(act_ref, dw_ref, c, col, tile, half, rows, shift, sums):
    taps = {}
    for rr in rows:
        for j in range(5):
            at = LEAD - 2 + j + col
            x = act_ref[c, rr - shift, at : at + tile, :]
            for o in range(half):
                q = (rr - o) * 5 + j
                if 0 <= rr - o < 5:
                    if q not in taps:
                        taps[q] = dw_ref[q : q + 1, c * LANES : (c + 1) * LANES]
                    v = x * taps[q]
                    sums[o] = v if sums[o] is None else sums[o] + v
    return sums


def near_body(states, emb_alls, dw_ref, act_refs, keep_ref, partial_ref, half, lon):
    for slot, (state, emb_all, act_ref) in enumerate(zip(states, emb_alls, act_refs)):
        chunks = emb_all.shape[1] // LANES
        turned = state[...].T
        for r in range(half):
            a = embed_row(turned, r, lon, emb_all[...])
            keep_ref[slot, r * lon : (r + 1) * lon, :] = a
            store_row(act_ref, r, a, lon)
    for slot, act_ref in enumerate(act_refs):
        for c in range(chunks):
            for k in range(lon // TILE):
                rows = range(2, 2 + half)
                sums = conv_tile(act_ref, dw_ref, c, k * TILE, TILE, half, rows, 2, [None] * half)
                for o in range(half):
                    partial_ref[slot, c, o, k * TILE : (k + 1) * TILE, :] = sums[o]


def near_first_kernel(
    half, idx_ref, own_ref, emb_ref, dw_ref, time_hbm, noise_hbm, traj_hbm,
    emb_all, coef_ref, keep_ref, partial_ref, g_own, g_send,
    act_ref, time_ref, noise_ref, traj_ref, sems,
):
    _, rows, _, lon = noise_ref.shape
    t, _, _, h = place()
    time_c = pltpu.make_async_copy(time_hbm, time_ref, sems.at[0])
    noise_c = pltpu.make_async_copy(noise_hbm, noise_ref, sems.at[1])
    time_c.start()
    noise_c.start()
    index = jnp.full((8, time_ref.shape[0] // 2), idx_ref[0], F32)
    time_c.wait()
    cond, level = condition_of(index, time_ref[...])
    coef_ref[...] = 0.125 * level[:, :LANES]
    fill_embedding(emb_all, emb_ref[...], cond[0:1, :])
    near_body((own_ref,), (emb_all,), dw_ref, (act_ref,), keep_ref, partial_ref, half, lon)
    noise_c.wait()
    scale = 0.125 * jnp.sqrt(level_of(jnp.full((1, lon), idx_ref[0], F32)))

    def emit(upper, anchored):
        for r in range(rows):
            value = scale * noise_ref[:, r, 0, :]
            if anchored:
                value = value + traj_ref[:, r, 0, :]
            cols = slice((r % half) * lon, (r % half + 1) * lon)
            target = g_own if (r < half) == upper else g_send
            target[:, cols] = value

    @pl.when(t == 0)
    def _():
        root = pltpu.make_async_copy(traj_hbm, traj_ref, sems.at[2])
        root.start()
        root.wait()

    for upper in (True, False):
        for anchored in (True, False):

            @pl.when((h == (0 if upper else 1)) & ((t == 0) == anchored))
            def _():
                emit(upper, anchored)


def near_later_kernel(half, lon, own_ref, part_ref, emb_own, emb_part, dw_ref, keep_ref, partial_ref, act0, act1):
    near_body((own_ref, part_ref), (emb_own, emb_part), dw_ref, (act0, act1), keep_ref, partial_ref, half, lon)


def spread_out(main, extra):
    done = 0
    for i, unit in enumerate(main):
        unit()
        while done < len(extra) and done * len(main) < (i + 1) * len(extra):
            extra[done]()
            done += 1
    for unit in extra[done:]:
        unit()


def finish(first_sum, second_sum, known, sent_ref, even_ref, rest):
    _, _, y, _ = place()
    even_ref[...] = jnp.where(y == 0, first_sum, second_sum)
    total = first_sum + second_sum
    if known is not None:
        total = total - known.astype(F32)
    sent_ref[...] = total.astype(BF16)
    for total_ref in rest:
        total_ref[...] = total


def finish_kernel(inc_own, drift_part, g_part, sent_ref, even_ref, *rest):
    finish(inc_own[...], drift_part[...] + g_part[...], None, sent_ref, even_ref, rest)


def far_kernel(first, staged, sizes, *refs):
    half, lon, chunks, ff, _ = sizes
    width = chunks * LANES
    refs = list(refs)

    def take(n):
        got = refs[:n]
        del refs[:n]
        return got

    if first:
        inner_own, outer_own, part5, outer_part = take(4)
        emb_own, coef_own, keep_in, partial, emb_ref, time_hbm = take(6)
    else:
        inner, outer = take(2)
        emb_own, emb_part, coef_own, coef_part, keep_in, partial, sent_in = take(7)
    dw_ref, gain_ref, up_ref, down_ref, out_ref, g_own = take(6)
    if first:
        inc_own, drift_part, emb_part, coef_part = take(4)
    else:
        (g_part,) = take(1)
        sent_ref, even_ref = take(2)
        rest = take(1) if staged else []
    act0, act1, conv_ref, norm_ref, up_out, hid_ref, bo_ref = take(7)
    if first:
        time_ref, time_sem = take(2)

    _, _, _, h = place()
    acts = (act0, act1)
    inside = 5 * (1 - h)
    outside = 5 * h
    near = 2 * lon
    whole = (False, first)
    if first:
        time_c = pltpu.make_async_copy(time_hbm, time_ref, time_sem)
        time_c.start()

    def condition_unit():
        quarter = width // 2
        row = lambda k: part5[PAD - k : PAD - k + 1, :quarter].astype(F32)
        index = jnp.broadcast_to(row(2) * 32.0 + row(1), (8, quarter))
        cond, level = condition_of(index, time_ref[...])
        coef_part[...] = 0.125 * level[:, :LANES]
        fill_embedding(emb_part, emb_ref[...], cond[0:1, :])

    def embed_units(slot):
        emb_all = (emb_own, emb_part)[slot]
        if not first:
            pieces = (
                (inner, slice((1 - slot) * near, (2 - slot) * near), inside),
                (outer, slice(slot * near, (slot + 1) * near), outside),
            )
        elif slot == 0:
            pieces = ((inner_own, slice(0, near), inside), (outer_own, slice(0, near), outside))
        else:
            pieces = ((part5, slice(0, (half + 2) * lon), 2 * (1 - h)), (outer_part, slice(0, near), outside))
        units = []
        for ref, cols, base in pieces:
            held = []

            def unit(r, ref=ref, cols=cols, base=base, held=held):
                if not held:
                    held.append(ref[:, cols].T)
                store_row(acts[slot], base + r, embed_row(held[0], r, lon, emb_all[...]), lon)

            units += [functools.partial(unit, r) for r in range((cols.stop - cols.start) // lon)]
        return units

    part = lon // 2

    def conv_units(b):
        slot, p = b // 2, b % 2
        flip = b % 2
        rows = range(half + 4) if whole[slot] else (0, 1, half + 2, half + 3)

        def tile_unit(c, k):
            col = p * part + k * TILE
            sums = [None if whole[slot] else partial[slot, c, o, col : col + TILE, :] for o in range(half)]
            sums = conv_tile(acts[slot], dw_ref, c, col, TILE, half, rows, 0, sums)
            for o in range(half):
                conv_ref[flip, c, o, k * TILE : (k + 1) * TILE, :] = sums[o]

        def norm_unit(o, k):
            span = slice(k * 48, (k + 1) * 48)
            x = [conv_ref[flip, c, o, span, :] for c in range(chunks)]
            mean = jnp.sum(functools.reduce(jnp.add, x), axis=1, keepdims=True) * (1.0 / width)
            x = [v - mean for v in x]
            var = jnp.sum(functools.reduce(jnp.add, [v * v for v in x]), axis=1, keepdims=True) * (1.0 / width)
            inv = lax.rsqrt(var + 1e-06)
            for c, v in enumerate(x):
                lane = slice(c * LANES, (c + 1) * LANES)
                value = (v * inv * gain_ref[:, lane]).astype(BF16)
                norm_ref[flip, o * part + k * 48 : o * part + (k + 1) * 48, lane] = value

        return [functools.partial(tile_unit, c, k) for c in range(chunks) for k in range(part // TILE)] + [
            functools.partial(norm_unit, o, k) for o in range(half) for k in range(part // 48)
        ]

    k0 = math.sqrt(2.0 / math.pi)

    def mix_units(b):
        slot, p = b // 2, b % 2
        flip = b % 2

        def up_unit(n):
            up_out[n % 2] = jnp.dot(norm_ref[flip], up_ref[:, n * 256 : (n + 1) * 256], preferred_element_type=F32)

        def gelu_unit(n, o):
            u = up_out[n % 2, o * part : (o + 1) * part, :]
            value = (u + u * jnp.tanh(u * (k0 + (k0 * 0.044715) * (u * u)))).astype(BF16)
            hid_ref[flip, o * part : (o + 1) * part, n * 256 : (n + 1) * 256] = value

        def down_unit(m):
            d = jnp.dot(hid_ref[flip], down_ref[:, m * 256 : (m + 1) * 256], preferred_element_type=F32)
            lane = slice(m * 256, (m + 1) * 256)
            for o in range(half):
                span = slice(o * lon + p * part, o * lon + (p + 1) * part)
                if whole[slot]:
                    c = 2 * m
                    at = slice(LEAD + p * part, LEAD + (p + 1) * part)
                    a = jnp.concatenate([acts[slot][c, 2 + o, at, :], acts[slot][c + 1, 2 + o, at, :]], axis=1)
                else:
                    a = keep_in[slot, span, lane].astype(F32)
                bo_ref[slot, span, lane] = (a + 0.5 * d[o * part : (o + 1) * part, :]).astype(BF16)

        steps = ff // 256
        units = [functools.partial(up_unit, 0)]
        for n in range(steps):
            if n + 1 < steps:
                units.append(functools.partial(up_unit, n + 1))
            units += [functools.partial(gelu_unit, n, o) for o in range(half)]
        return units + [functools.partial(down_unit, m) for m in range(width // 256)]

    incs = []

    def out_unit(slot):
        drift = lax.dot_general(out_ref[...], bo_ref[slot], (((1,), (1,)), ((), ())), preferred_element_type=F32)
        drift = (coef_own, coef_part)[slot][0:1, 0:1] * drift
        if slot == 0:
            drift = drift + g_own[...]
        elif not first:
            drift = drift + g_part[...]
        if first:
            (inc_own, drift_part)[slot][...] = drift
        else:
            incs.append(drift)

    for unit in embed_units(0):
        unit()
    if first:
        spread_out(conv_units(0), [])
        time_c.wait()
        condition_unit()
        spread_out(conv_units(1), embed_units(1) + mix_units(0))
    else:
        spread_out(conv_units(0), embed_units(1))
        spread_out(conv_units(1), mix_units(0))
    spread_out(conv_units(2), mix_units(1))
    spread_out(conv_units(3), mix_units(2) + [functools.partial(out_unit, 0)])
    for unit in mix_units(3):
        unit()
    out_unit(1)
    if not first:
        finish(incs[0], incs[1], sent_in[...], sent_ref, even_ref, rest)


def cost(flops, nbytes=1 << 20):
    return pl.CostEstimate(flops=int(flops), bytes_accessed=nbytes, transcendentals=0)


def act_scratch(chunks, rows, lon):
    return pltpu.VMEM((chunks, rows, lon + 2 * LEAD, LANES), F32)


def far(first, staged, head, weights, half, lon):
    _, _, up, _, _, g_own = weights[:6]
    channels, points = g_own.shape
    width, ff = up.shape
    chunks = width // LANES
    block = points // 2
    grid = ((channels, points), F32)
    outs = [grid, grid] if first else [((channels, points), BF16), grid] + [grid] * staged
    specs = [VMEM] * (len(head) + len(weights))
    scratch = [act_scratch(chunks, half + 4, lon)] * 2 + [
        pltpu.VMEM((2, chunks, half, lon // 2, LANES), F32),
        pltpu.VMEM((2, block, width), BF16),
        pltpu.VMEM((2, block, 256), F32),
        pltpu.VMEM((2, block, ff), BF16),
        pltpu.VMEM((2, points, width), BF16),
    ]
    if first:
        outs += [((PAD, width), BF16), ((8, LANES), F32)]
        specs[len(head) - 1] = HBM
        scratch += [pltpu.VMEM(head[-1].shape, F32), pltpu.SemaphoreType.DMA]
    return call(
        functools.partial(far_kernel, first, staged, (half, lon, chunks, ff, channels)),
        outs,
        (*head, *weights),
        specs,
        scratch,
        cost(2 * 2 * points * width * (channels * 2 + 2 * ff + 25)),
    )


def middle_kernel(count, lon, *refs):
    gots, refs = refs[:count], refs[count:]
    even, own3, part5, sum_ref, own_ref, part_ref, inner_ref, outer_ref = refs
    channels, points = even.shape
    t, _, y, h = place()
    near = 2 * lon
    total = gots[0][...].astype(F32)
    for g in gots[1:]:
        total = total + g[...].astype(F32)
    sum_ref[...] = total
    odd = (total + even[...]).astype(BF16)
    flat = total.astype(BF16)
    for ref in (own_ref, part_ref, inner_ref, outer_ref):
        ref[channels:, :] = jnp.ones((PAD - channels, ref.shape[1]), BF16)

    def emit(parity, upper):
        shift = 0 if upper else near
        start = own3[:channels, :] if parity == 0 else part5[:channels, shift : shift + points]
        state = jnp.where(t < 2, start.astype(F32), flat.astype(F32)).astype(BF16)
        pair = (state, odd) if parity == 0 else (odd, state)
        own_ref[:channels, :] = pair[0]
        part_ref[:channels, :] = pair[1]
        for k, s in enumerate(pair):
            cols = slice(k * near, (k + 1) * near)
            low, high = s[:, :near], s[:, points - near :]
            inner_ref[:channels, cols] = high if upper else low
            outer_ref[:channels, cols] = low if upper else high

    for parity in range(2):
        for half_at in range(2):

            @pl.when((y == parity) & (h == half_at))
            def _():
                emit(parity, half_at == 0)


def ending_kernel(count, *refs):
    gots, (before, even, mine_ref, send_ref) = refs[:count], refs[count:]
    _, _, y, _ = place()
    total = before[...]
    for g in gots:
        total = total + g[...].astype(F32)
    odd = total + even[...]
    mine_ref[...] = jnp.where(y == 0, total, odd)
    send_ref[...] = jnp.where(y == 0, odd, total)


def output_kernel(mine, other, traj_hbm, out_ref, sem):
    _, rows, _, lon = out_ref.shape
    half = rows // 2
    t, _, _, h = place()

    def emit(upper):
        for r in range(rows):
            cols = slice((r % half) * lon, (r % half + 1) * lon)
            out_ref[:, r, 0, :] = (mine if (r < half) == upper else other)[:, cols]

    @pl.when((h == 0) & (t > 0))
    def _():
        emit(True)

    @pl.when((h == 1) & (t > 0))
    def _():
        emit(False)

    @pl.when(t == 0)
    def _():
        copy = pltpu.make_async_copy(traj_hbm, out_ref, sem)
        copy.start()
        copy.wait()


def call(body, outs, ins, specs=None, scratch=(), estimate=None):
    return pl.pallas_call(
        body,
        out_shape=tuple(jax.ShapeDtypeStruct(s, d) for s, d in outs),
        in_specs=specs or [VMEM] * len(ins),
        out_specs=tuple([VMEM] * len(outs)),
        scratch_shapes=list(scratch),
        compiler_params=LIMIT,
        cost_estimate=estimate,
    )(*ins)


def exchange(sent, total=None, *, groups, memory):
    gots, kept = [], []
    base, moved, unit = sent, None, 1
    while unit < groups:
        if unit > 1:
            rest = memory[len(kept)] if memory else 0.0
            sent = (total + moved + rest).astype(BF16)
            kept.append(base.astype(F32) + moved + rest - sent.astype(F32))
        for step in range(1, RADIX):
            shift = 2 * step * unit
            if shift < 2 * groups:
                gots.append(lax.ppermute(sent, "tm", [(i, i + shift) for i in range(2 * groups - shift)]))
        unit *= RADIX
        if groups > RADIX:
            moved = functools.reduce(jnp.add, [g.astype(F32) for g in gots])
    return gots, kept


def shards(
    traj, noise, step_index, embed_weight, time_weight, dw_weight, ln_gain, up_weight, down_weight, out_weight,
):
    times, bands = lax.axis_size("tm"), lax.axis_size("lat")
    groups = times // 2
    channels, rows, lon = traj.shape[1:]
    half = rows // 2
    width = embed_weight.shape[1]
    points, span, near = half * lon, (half + 2) * lon, 2 * lon
    axes = ("tm", "lat")

    def at(a, b):
        return a * bands + b

    cells = [(a, b, (a + b) % 2) for a in range(times) for b in range(bands)]
    swap = [(at(a, b), at(a ^ 1, b)) for a, b, _ in cells]
    side = [(at(a, b), at(a, b + (1 if c else -1))) for a, b, c in cells if 0 <= b + (1 if c else -1) < bands]
    cross = [(at(a, b), at(a ^ 1, b + (-1 if c else 1))) for a, b, c in cells if 0 <= b + (-1 if c else 1) < bands]

    root = traj.reshape(channels, rows, 1, lon)
    draws = noise.reshape(channels, rows, 1, lon)
    band = (channels, rows, 1, lon)
    chunks = width // LANES
    own3, inner_own, to_swap, to_side, to_cross = call(
        prep_kernel,
        [((PAD, points), BF16), ((PAD, near), BF16), ((PAD, span), BF16), ((PAD, near), BF16), ((PAD, near), BF16)],
        (step_index, root),
        [SMEM, HBM],
        [pltpu.VMEM(band, F32), pltpu.VMEM((PAD, rows * lon), BF16), pltpu.SemaphoreType.DMA],
        cost(1e9),
    )
    part5 = lax.ppermute(to_swap, axes, swap)
    outer_part = lax.ppermute(to_cross, axes, cross)
    outer_own = lax.ppermute(to_side, axes, side)
    dw = dw_weight.T
    work = 2 * points * width * (2 * channels + 25)

    def kept(slots):
        return [((slots, points, width), BF16), ((slots, chunks, half, lon, LANES), F32)]

    emb_own, coef_own, keep, partial, g_own, g_send = call(
        functools.partial(near_first_kernel, half),
        [((PAD, width), BF16), ((8, LANES), F32)] + kept(1) + [((channels, points), F32)] * 2,
        (step_index, own3, embed_weight, dw, time_weight, draws, root),
        [SMEM, VMEM, VMEM, VMEM, HBM, HBM, HBM],
        [
            act_scratch(chunks, half, lon),
            pltpu.VMEM(time_weight.shape, F32),
            pltpu.VMEM(band, F32),
            pltpu.VMEM(band, F32),
            pltpu.SemaphoreType.DMA((3,)),
        ],
        cost(20 * work),
    )
    g_part = lax.ppermute(g_send, axes, swap)
    weights = (dw, ln_gain.reshape(1, width), up_weight, down_weight, out_weight.T, g_own)
    staged = groups > RADIX
    inc_own, drift_part, emb_part, coef_part = far(
        True,
        staged,
        (inner_own, outer_own, part5, outer_part, emb_own, coef_own, keep, partial, embed_weight, time_weight),
        weights,
        half,
        lon,
    )
    sums = [((channels, points), BF16)] + [((channels, points), F32)] * (1 + staged)
    sent, even, *total = call(finish_kernel, sums, (inc_own, drift_part, g_part))
    gots, memory = exchange(sent, *total, groups=groups, memory=None)
    before = None
    for _ in range(1, ITERS):
        before, s_own, s_part, inner, outer = call(
            functools.partial(middle_kernel, len(gots), lon),
            [((channels, points), F32)] + [((PAD, points), BF16)] * 2 + [((PAD, 2 * near), BF16)] * 2,
            (*gots, even, own3, part5),
        )
        inner = lax.ppermute(inner, axes, swap)
        outer = lax.ppermute(outer, axes, side)
        keep, partial = call(
            functools.partial(near_later_kernel, half, lon),
            kept(2),
            (s_own, s_part, emb_own, emb_part, dw),
            scratch=[act_scratch(chunks, half, lon)] * 2,
            estimate=cost(20 * work),
        )
        sent, even, *total = far(
            False,
            staged,
            (inner, outer, emb_own, emb_part, coef_own, coef_part, keep, partial, sent),
            weights + (g_part,),
            half,
            lon,
        )
        gots, memory = exchange(sent, *total, groups=groups, memory=memory)
    mine, send = call(
        functools.partial(ending_kernel, len(gots)), [((channels, points), F32)] * 2, (*gots, before, even)
    )
    other = lax.ppermute(send, axes, swap)
    (result,) = call(output_kernel, [(band, F32)], (mine, other, root), [VMEM, VMEM, HBM], [pltpu.SemaphoreType.DMA])
    return result.reshape(1, channels, rows, lon)


def solution(mesh):
    in_specs = (P("tm", None, "lat", None), P("tm", None, "lat", None), P("tm")) + (P(),) * 7
    out_specs = P("tm", None, "lat", None)

    return jax.shard_map(shards, mesh=mesh, in_specs=in_specs, out_specs=out_specs, check_vma=False)
```

```python
import functools
import math

import jax
import jax.numpy as jnp
from jax import lax
from jax.experimental import pallas as pl
from jax.experimental.pallas import tpu as pltpu
from jax.sharding import PartitionSpec as P


ITERS = 2
LEVELS = 1000
LANES = 128
LEAD = 8
RADIX = 4
TILE = 24
BF16 = jnp.bfloat16
F32 = jnp.float32
VMEM = pl.BlockSpec(memory_space=pltpu.VMEM)
SMEM = pl.BlockSpec(memory_space=pltpu.SMEM)
HBM = pl.BlockSpec(memory_space=pltpu.HBM)
VMEM_OR_HBM = pl.BlockSpec(memory_space=pl.ANY)
PAD = 88
LIMIT = pltpu.CompilerParams(vmem_limit_bytes=24 << 20)


def place():
    t, l = lax.axis_index("tm"), lax.axis_index("lat")
    return t, l, t % 2, (t + l) % 2


def level_of(index):
    return 2.0 * jnp.exp(index * (math.log(0.1) / (LEVELS - 1)))


def prep_kernel(idx_ref, traj_hbm, own_ref, inner_ref, swap_ref, side_ref, traj_ref, v_ref, sem):
    channels, rows, _, lon = traj_ref.shape
    half = rows // 2
    _, _, _, h = place()
    copy = pltpu.make_async_copy(traj_hbm, traj_ref, sem)
    copy.start()
    v_ref[channels:, :] = jnp.ones((PAD - channels, rows * lon), BF16)
    copy.wait()
    for r in range(rows):
        v_ref[:channels, r * lon : (r + 1) * lon] = traj_ref[:, r, 0, :].astype(BF16)
    span, near = (half + 2) * lon, 2 * lon

    def cut(upper):
        low, high = v_ref[:, :span], v_ref[:, lon : lon + span]
        first, last = v_ref[:, :near], v_ref[:, (rows - 2) * lon :]
        own_ref[...] = v_ref[:, : half * lon] if upper else v_ref[:, half * lon :]
        inner_ref[...] = v_ref[:, half * lon : span] if upper else v_ref[:, lon : half * lon]
        swap_ref[...] = high if upper else low
        side_ref[...] = first if upper else last

    @pl.when(h == 0)
    def _():
        cut(True)

    @pl.when(h == 1)
    def _():
        cut(False)

    index = idx_ref[0]
    swap_ref[PAD - 2 : PAD - 1, :] = jnp.full((1, span), index // 32, F32).astype(BF16)
    swap_ref[PAD - 1 : PAD, :] = jnp.full((1, span), index % 32, F32).astype(BF16)


def condition_of(index, time_weight):
    half_width = index.shape[1]
    level = level_of(index)
    step = lax.broadcasted_iota(jnp.int32, index.shape, 1).astype(F32)
    angle = jnp.log(level) * jnp.exp(step * (-math.log(100.0) / half_width))
    features = jnp.concatenate([jnp.cos(angle), jnp.sin(angle)], axis=1)
    z = jnp.dot(features, time_weight, precision=lax.Precision.HIGHEST, preferred_element_type=F32)
    return z / (1.0 + jnp.exp(-z)), level


def fill_embedding(all_ref, emb, cond):
    channels, width = emb.shape
    all_ref[:channels, :] = emb
    all_ref[channels:, :] = jnp.zeros((PAD - channels, width), BF16)
    rest = cond
    for k in range(3):
        piece = rest.astype(BF16)
        all_ref[channels + k : channels + k + 1, :] = piece
        rest = rest - piece.astype(F32)


def embed_row(turned, r, lon, emb_all):
    return jnp.dot(turned[r * lon : (r + 1) * lon, :], emb_all, preferred_element_type=F32).astype(BF16)


def store_row(act_ref, row, a, lon):
    a = a.astype(F32)
    for c in range(a.shape[1] // LANES):
        piece = a[:, c * LANES : (c + 1) * LANES]
        act_ref[c, row, LEAD : LEAD + lon, :] = piece
        act_ref[c, row, 0:LEAD, :] = piece[lon - LEAD : lon, :]
        act_ref[c, row, LEAD + lon : 2 * LEAD + lon, :] = piece[0:LEAD, :]


def conv_tile(act_ref, dw_ref, c, col, tile, half, rows, shift, sums):
    taps = {}
    for rr in rows:
        for j in range(5):
            at = LEAD - 2 + j + col
            x = act_ref[c, rr - shift, at : at + tile, :]
            for o in range(half):
                q = (rr - o) * 5 + j
                if 0 <= rr - o < 5:
                    if q not in taps:
                        taps[q] = dw_ref[q : q + 1, c * LANES : (c + 1) * LANES]
                    v = x * taps[q]
                    sums[o] = v if sums[o] is None else sums[o] + v
    return sums


def near_body(states, emb_alls, dw_ref, act_refs, keep_ref, partial_ref, half, lon):
    for slot, (state, emb_all, act_ref) in enumerate(zip(states, emb_alls, act_refs)):
        chunks = emb_all.shape[1] // LANES
        turned = state[...].T
        for r in range(half):
            a = embed_row(turned, r, lon, emb_all[...])
            keep_ref[slot, r * lon : (r + 1) * lon, :] = a
            store_row(act_ref, r, a, lon)
    for slot, act_ref in enumerate(act_refs):
        for c in range(chunks):
            for k in range(lon // TILE):
                rows = range(2, 2 + half)
                sums = conv_tile(act_ref, dw_ref, c, k * TILE, TILE, half, rows, 2, [None] * half)
                for o in range(half):
                    partial_ref[slot, c, o, k * TILE : (k + 1) * TILE, :] = sums[o]


def near_first_kernel(
    half, idx_ref, own_ref, emb_ref, dw_ref, time_hbm, noise_hbm, traj_hbm,
    emb_all, coef_ref, keep_ref, partial_ref, g_own, g_send,
    act_ref, time_ref, noise_ref, traj_ref, sems,
):
    _, rows, _, lon = noise_ref.shape
    t, _, _, h = place()
    time_c = pltpu.make_async_copy(time_hbm, time_ref, sems.at[0])
    noise_c = pltpu.make_async_copy(noise_hbm, noise_ref, sems.at[1])
    time_c.start()
    noise_c.start()
    index = jnp.full((8, time_ref.shape[0] // 2), idx_ref[0], F32)
    time_c.wait()
    cond, level = condition_of(index, time_ref[...])
    coef_ref[...] = 0.125 * level[:, :LANES]
    fill_embedding(emb_all, emb_ref[...], cond[0:1, :])
    near_body((own_ref,), (emb_all,), dw_ref, (act_ref,), keep_ref, partial_ref, half, lon)
    noise_c.wait()
    scale = 0.125 * jnp.sqrt(level_of(jnp.full((1, lon), idx_ref[0], F32)))

    def emit(upper, anchored):
        for r in range(rows):
            value = scale * noise_ref[:, r, 0, :]
            if anchored:
                value = value + traj_ref[:, r, 0, :]
            cols = slice((r % half) * lon, (r % half + 1) * lon)
            target = g_own if (r < half) == upper else g_send
            target[:, cols] = value

    @pl.when(t == 0)
    def _():
        root = pltpu.make_async_copy(traj_hbm, traj_ref, sems.at[2])
        root.start()
        root.wait()

    for upper in (True, False):
        for anchored in (True, False):

            @pl.when((h == (0 if upper else 1)) & ((t == 0) == anchored))
            def _():
                emit(upper, anchored)


def near_later_kernel(half, lon, own_ref, part_ref, emb_own, emb_part, dw_ref, keep_ref, partial_ref, act0, act1):
    near_body((own_ref, part_ref), (emb_own, emb_part), dw_ref, (act0, act1), keep_ref, partial_ref, half, lon)


def spread_out(main, extra):
    done = 0
    for i, unit in enumerate(main):
        unit()
        while done < len(extra) and done * len(main) < (i + 1) * len(extra):
            extra[done]()
            done += 1
    for unit in extra[done:]:
        unit()


def pack(ref, value):
    channels, points = value.shape
    for k in range(PAD // 8):
        piece = value[8 * k : min(8 * k + 8, channels), :]
        ref[: piece.shape[0], k * points : (k + 1) * points] = piece.astype(ref.dtype)


def unpack(ref, channels, points, start=0, count=None):
    count = points if count is None else count
    pieces = []
    for k in range(PAD // 8):
        at = k * points + start
        pieces.append(ref[: min(8, channels - 8 * k), at : at + count].astype(F32))
    return jnp.concatenate(pieces, axis=0)


def packed(points, dtype):
    return ((8, PAD // 8 * points), dtype)


def finish(first_sum, second_sum, known, sent_ref, even_ref, rest):
    _, _, y, _ = place()
    even_ref[...] = jnp.where(y == 0, first_sum, second_sum)
    total = first_sum + second_sum
    if known is not None:
        total = total - unpack(known, *total.shape)
    pack(sent_ref, total)
    for total_ref in rest:
        pack(total_ref, total)


def finish_kernel(inc_own, drift_part, g_part, sent_ref, even_ref, *rest):
    finish(inc_own[...], drift_part[...] + g_part[...], None, sent_ref, even_ref, rest)


def far_kernel(first, staged, sizes, *refs):
    half, lon, chunks, ff, _ = sizes
    width = chunks * LANES
    refs = list(refs)

    def take(n):
        got = refs[:n]
        del refs[:n]
        return got

    if first:
        inner_own, part5, outer = take(3)
        emb_own, coef_own, keep_in, partial, emb_ref, time_hbm = take(6)
    else:
        inner, outer = take(2)
        emb_own, emb_part, coef_own, coef_part, keep_in, partial, sent_in = take(7)
    dw_ref, gain_ref, up_ref, down_ref, out_ref, g_own = take(6)
    if first:
        inc_own, drift_part, emb_part, coef_part = take(4)
    else:
        (g_part,) = take(1)
        sent_ref, even_ref = take(2)
        rest = take(1) if staged else []
    act0, act1, conv_ref, norm_ref, up_out, hid_ref, bo_ref = take(7)
    if first:
        time_ref, time_sem = take(2)

    _, _, _, h = place()
    acts = (act0, act1)
    inside = 5 * (1 - h)
    outside = 5 * h
    near = 2 * lon
    whole = (False, first)
    if first:
        time_c = pltpu.make_async_copy(time_hbm, time_ref, time_sem)
        time_c.start()

    def condition_unit():
        quarter = width // 2
        row = lambda k: part5[PAD - k : PAD - k + 1, :quarter].astype(F32)
        index = jnp.broadcast_to(row(2) * 32.0 + row(1), (8, quarter))
        cond, level = condition_of(index, time_ref[...])
        coef_part[...] = 0.125 * level[:, :LANES]
        fill_embedding(emb_part, emb_ref[...], cond[0:1, :])

    def embed_units(slot):
        emb_all = (emb_own, emb_part)[slot]
        if not first:
            pieces = (
                (inner, slice((1 - slot) * near, (2 - slot) * near), inside),
                (outer, slice(slot * near, (slot + 1) * near), outside),
            )
        elif slot == 0:
            pieces = ((inner_own, slice(0, near), inside), (outer, slice(0, near), outside))
        else:
            pieces = ((part5, slice(0, (half + 2) * lon), 2 * (1 - h)), (outer, slice(near, 2 * near), outside))
        units = []
        for ref, cols, base in pieces:
            held = []

            def unit(r, ref=ref, cols=cols, base=base, held=held):
                if not held:
                    held.append(ref[:, cols].T)
                store_row(acts[slot], base + r, embed_row(held[0], r, lon, emb_all[...]), lon)

            units += [functools.partial(unit, r) for r in range((cols.stop - cols.start) // lon)]
        return units

    part = lon // 2

    def conv_units(b):
        slot, p = b // 2, b % 2
        flip = b % 2
        rows = range(half + 4) if whole[slot] else (0, 1, half + 2, half + 3)

        def tile_unit(c, k):
            col = p * part + k * TILE
            sums = [None if whole[slot] else partial[slot, c, o, col : col + TILE, :] for o in range(half)]
            sums = conv_tile(acts[slot], dw_ref, c, col, TILE, half, rows, 0, sums)
            for o in range(half):
                conv_ref[flip, c, o, k * TILE : (k + 1) * TILE, :] = sums[o]

        def norm_unit(o, k):
            span = slice(k * 48, (k + 1) * 48)
            x = [conv_ref[flip, c, o, span, :] for c in range(chunks)]
            mean = jnp.sum(functools.reduce(jnp.add, x), axis=1, keepdims=True) * (1.0 / width)
            x = [v - mean for v in x]
            var = jnp.sum(functools.reduce(jnp.add, [v * v for v in x]), axis=1, keepdims=True) * (1.0 / width)
            inv = lax.rsqrt(var + 1e-06)
            for c, v in enumerate(x):
                lane = slice(c * LANES, (c + 1) * LANES)
                value = (v * inv * gain_ref[:, lane]).astype(BF16)
                norm_ref[flip, o * part + k * 48 : o * part + (k + 1) * 48, lane] = value

        return [functools.partial(tile_unit, c, k) for c in range(chunks) for k in range(part // TILE)] + [
            functools.partial(norm_unit, o, k) for o in range(half) for k in range(part // 48)
        ]

    k0 = math.sqrt(2.0 / math.pi)

    def mix_units(b):
        slot, p = b // 2, b % 2
        flip = b % 2

        def up_unit(n):
            up_out[n % 2] = jnp.dot(norm_ref[flip], up_ref[:, n * 256 : (n + 1) * 256], preferred_element_type=F32)

        def gelu_unit(n, o):
            u = up_out[n % 2, o * part : (o + 1) * part, :]
            value = (u + u * jnp.tanh(u * (k0 + (k0 * 0.044715) * (u * u)))).astype(BF16)
            hid_ref[flip, o * part : (o + 1) * part, n * 256 : (n + 1) * 256] = value

        def down_unit(m):
            d = jnp.dot(hid_ref[flip], down_ref[:, m * 256 : (m + 1) * 256], preferred_element_type=F32)
            lane = slice(m * 256, (m + 1) * 256)
            for o in range(half):
                span = slice(o * lon + p * part, o * lon + (p + 1) * part)
                if whole[slot]:
                    c = 2 * m
                    at = slice(LEAD + p * part, LEAD + (p + 1) * part)
                    a = jnp.concatenate([acts[slot][c, 2 + o, at, :], acts[slot][c + 1, 2 + o, at, :]], axis=1)
                else:
                    a = keep_in[slot, span, lane].astype(F32)
                bo_ref[slot, span, lane] = (a + 0.5 * d[o * part : (o + 1) * part, :]).astype(BF16)

        steps = ff // 256
        units = [functools.partial(up_unit, 0)]
        for n in range(steps):
            if n + 1 < steps:
                units.append(functools.partial(up_unit, n + 1))
            units += [functools.partial(gelu_unit, n, o) for o in range(half)]
        return units + [functools.partial(down_unit, m) for m in range(width // 256)]

    incs = []

    def out_unit(slot):
        drift = lax.dot_general(out_ref[...], bo_ref[slot], (((1,), (1,)), ((), ())), preferred_element_type=F32)
        drift = (coef_own, coef_part)[slot][0:1, 0:1] * drift
        if slot == 0:
            drift = drift + g_own[...]
        elif not first:
            drift = drift + g_part[...]
        if first:
            (inc_own, drift_part)[slot][...] = drift
        else:
            incs.append(drift)

    for unit in embed_units(0):
        unit()
    if first:
        spread_out(conv_units(0), [])
        time_c.wait()
        condition_unit()
        spread_out(conv_units(1), embed_units(1) + mix_units(0))
    else:
        spread_out(conv_units(0), embed_units(1))
        spread_out(conv_units(1), mix_units(0))
    spread_out(conv_units(2), mix_units(1))
    spread_out(conv_units(3), mix_units(2) + [functools.partial(out_unit, 0)])
    for unit in mix_units(3):
        unit()
    out_unit(1)
    if not first:
        finish(incs[0], incs[1], sent_in, sent_ref, even_ref, rest)


def cost(flops, nbytes=1 << 20):
    return pl.CostEstimate(flops=int(flops), bytes_accessed=nbytes, transcendentals=0)


def act_scratch(chunks, rows, lon):
    return pltpu.VMEM((chunks, rows, lon + 2 * LEAD, LANES), F32)


def far(first, staged, head, weights, half, lon):
    _, _, up, _, _, g_own = weights[:6]
    channels, points = g_own.shape
    width, ff = up.shape
    chunks = width // LANES
    block = points // 2
    grid = ((channels, points), F32)
    outs = [grid, grid] if first else [packed(points, BF16), grid] + [packed(points, F32)] * staged
    specs = [VMEM] * (len(head) + len(weights))
    scratch = [act_scratch(chunks, half + 4, lon)] * 2 + [
        pltpu.VMEM((2, chunks, half, lon // 2, LANES), F32),
        pltpu.VMEM((2, block, width), BF16),
        pltpu.VMEM((2, block, 256), F32),
        pltpu.VMEM((2, block, ff), BF16),
        pltpu.VMEM((2, points, width), BF16),
    ]
    if first:
        outs += [((PAD, width), BF16), ((8, LANES), F32)]
        specs[len(head) - 1] = HBM
        scratch += [pltpu.VMEM(head[-1].shape, F32), pltpu.SemaphoreType.DMA]
    return call(
        functools.partial(far_kernel, first, staged, (half, lon, chunks, ff, channels)),
        outs,
        (*head, *weights),
        specs,
        scratch,
        cost(2 * 2 * points * width * (channels * 2 + 2 * ff + 25)),
    )


def edges_kernel(near, own_ref, part_ref, out_ref):
    _, _, _, h = place()
    out_ref[:, :near] = own_ref[...]

    @pl.when(h == 0)
    def _():
        out_ref[:, near:] = part_ref[:, :near]

    @pl.when(h == 1)
    def _():
        out_ref[:, near:] = part_ref[:, part_ref.shape[1] - near :]


def middle_kernel(count, lon, *refs):
    gots, refs = refs[:count], refs[count:]
    even, own3, part5, sum_ref, own_ref, part_ref, inner_ref, outer_ref = refs
    channels, points = even.shape
    t, _, y, h = place()
    near = 2 * lon
    total = unpack(gots[0], channels, points)
    for g in gots[1:]:
        total = total + unpack(g, channels, points)
    sum_ref[...] = total
    odd = (total + even[...]).astype(BF16)
    flat = total.astype(BF16)
    for ref in (own_ref, part_ref, inner_ref, outer_ref):
        ref[channels:, :] = jnp.ones((PAD - channels, ref.shape[1]), BF16)

    def emit(parity, upper):
        shift = 0 if upper else near
        start = own3[:channels, :] if parity == 0 else part5[:channels, shift : shift + points]
        state = jnp.where(t < 2, start.astype(F32), flat.astype(F32)).astype(BF16)
        pair = (state, odd) if parity == 0 else (odd, state)
        own_ref[:channels, :] = pair[0]
        part_ref[:channels, :] = pair[1]
        for k, s in enumerate(pair):
            cols = slice(k * near, (k + 1) * near)
            low, high = s[:, :near], s[:, points - near :]
            inner_ref[:channels, cols] = high if upper else low
            outer_ref[:channels, cols] = low if upper else high

    for parity in range(2):
        for half_at in range(2):

            @pl.when((y == parity) & (h == half_at))
            def _():
                emit(parity, half_at == 0)


def ending_kernel(count, *refs):
    gots, (before, even, mine_ref, send_ref) = refs[:count], refs[count:]
    _, _, y, _ = place()
    total = before[...]
    for g in gots:
        total = total + unpack(g, *total.shape)
    odd = total + even[...]
    mine_ref[...] = jnp.where(y == 0, total, odd)
    pack(send_ref, jnp.where(y == 0, odd, total))


def output_kernel(mine, other, traj_hbm, out_ref, sem):
    channels, rows, _, lon = out_ref.shape
    half = rows // 2
    t, _, _, h = place()

    def emit(upper):
        for r in range(rows):
            start = (r % half) * lon
            if (r < half) == upper:
                out_ref[:, r, 0, :] = mine[:, start : start + lon]
            else:
                out_ref[:, r, 0, :] = unpack(other, channels, half * lon, start, lon)

    @pl.when((h == 0) & (t > 0))
    def _():
        emit(True)

    @pl.when((h == 1) & (t > 0))
    def _():
        emit(False)

    @pl.when(t == 0)
    def _():
        copy = pltpu.make_async_copy(traj_hbm, out_ref, sem)
        copy.start()
        copy.wait()


def call(body, outs, ins, specs=None, scratch=(), estimate=None):
    return pl.pallas_call(
        body,
        out_shape=tuple(jax.ShapeDtypeStruct(s, d) for s, d in outs),
        in_specs=specs or [VMEM] * len(ins),
        out_specs=tuple([VMEM] * len(outs)),
        scratch_shapes=list(scratch),
        compiler_params=LIMIT,
        cost_estimate=estimate,
    )(*ins)


def exchange(sent, total=None, *, groups, memory):
    gots, kept = [], []
    base, moved, unit = sent, None, 1
    while unit < groups:
        if unit > 1:
            rest = memory[len(kept)] if memory else 0.0
            sent = (total + moved + rest).astype(BF16)
            kept.append(base.astype(F32) + moved + rest - sent.astype(F32))
        for step in range(1, RADIX):
            shift = 2 * step * unit
            if shift < 2 * groups:
                gots.append(lax.ppermute(sent, "tm", [(i, i + shift) for i in range(2 * groups - shift)]))
        unit *= RADIX
        if groups > RADIX:
            moved = functools.reduce(jnp.add, [g.astype(F32) for g in gots])
    return gots, kept


def shards(
    traj, noise, step_index, embed_weight, time_weight, dw_weight, ln_gain, up_weight, down_weight, out_weight,
):
    times, bands = lax.axis_size("tm"), lax.axis_size("lat")
    groups = times // 2
    channels, rows, lon = traj.shape[1:]
    half = rows // 2
    width = embed_weight.shape[1]
    points, span, near = half * lon, (half + 2) * lon, 2 * lon
    axes = ("tm", "lat")

    def at(a, b):
        return a * bands + b

    cells = [(a, b, (a + b) % 2) for a in range(times) for b in range(bands)]
    swap = [(at(a, b), at(a ^ 1, b)) for a, b, _ in cells]
    side = [(at(a, b), at(a, b + (1 if c else -1))) for a, b, c in cells if 0 <= b + (1 if c else -1) < bands]

    root = traj.reshape(channels, rows, 1, lon)
    draws = noise.reshape(channels, rows, 1, lon)
    band = (channels, rows, 1, lon)
    chunks = width // LANES
    own3, inner_own, to_swap, to_side = call(
        prep_kernel,
        [((PAD, points), BF16), ((PAD, near), BF16), ((PAD, span), BF16), ((PAD, near), BF16)],
        (step_index, root),
        [SMEM, HBM],
        [pltpu.VMEM(band, F32), pltpu.VMEM((PAD, rows * lon), BF16), pltpu.SemaphoreType.DMA],
        cost(1e9),
    )
    part5 = lax.ppermute(to_swap, axes, swap)
    dw = dw_weight.T
    work = 2 * points * width * (2 * channels + 25)

    def kept(slots):
        return [((slots, points, width), BF16), ((slots, chunks, half, lon, LANES), F32)]

    emb_own, coef_own, keep, partial, g_own, g_send = call(
        functools.partial(near_first_kernel, half),
        [((PAD, width), BF16), ((8, LANES), F32)] + kept(1) + [((channels, points), F32)] * 2,
        (step_index, own3, embed_weight, dw, time_weight, draws, root),
        [SMEM, VMEM, VMEM, VMEM, HBM, HBM, HBM],
        [
            act_scratch(chunks, half, lon),
            pltpu.VMEM(time_weight.shape, F32),
            pltpu.VMEM(band, F32),
            pltpu.VMEM(band, F32),
            pltpu.SemaphoreType.DMA((3,)),
        ],
        cost(20 * work),
    )
    (to_side,) = call(functools.partial(edges_kernel, near), [((PAD, 2 * near), BF16)], (to_side, part5))
    outer = lax.ppermute(to_side, axes, side)
    g_part = lax.ppermute(g_send, axes, swap)
    weights = (dw, ln_gain.reshape(1, width), up_weight, down_weight, out_weight.T, g_own)
    staged = groups > RADIX
    inc_own, drift_part, emb_part, coef_part = far(
        True,
        staged,
        (inner_own, part5, outer, emb_own, coef_own, keep, partial, embed_weight, time_weight),
        weights,
        half,
        lon,
    )
    sums = [packed(points, BF16), ((channels, points), F32)] + [packed(points, F32)] * staged
    sent, even, *total = call(finish_kernel, sums, (inc_own, drift_part, g_part))
    gots, memory = exchange(sent, *total, groups=groups, memory=None)
    before = None
    for _ in range(1, ITERS):
        before, s_own, s_part, inner, outer = call(
            functools.partial(middle_kernel, len(gots), lon),
            [((channels, points), F32)] + [((PAD, points), BF16)] * 2 + [((PAD, 2 * near), BF16)] * 2,
            (*gots, even, own3, part5),
        )
        inner = lax.ppermute(inner, axes, swap)
        outer = lax.ppermute(outer, axes, side)
        keep, partial = call(
            functools.partial(near_later_kernel, half, lon),
            kept(2),
            (s_own, s_part, emb_own, emb_part, dw),
            scratch=[act_scratch(chunks, half, lon)] * 2,
            estimate=cost(20 * work),
        )
        sent, even, *total = far(
            False,
            staged,
            (inner, outer, emb_own, emb_part, coef_own, coef_part, keep, partial, sent),
            weights + (g_part,),
            half,
            lon,
        )
        gots, memory = exchange(sent, *total, groups=groups, memory=memory)
    mine, send = call(
        functools.partial(ending_kernel, len(gots)),
        [((channels, points), F32), packed(points, F32)],
        (*gots, before, even),
    )
    other = lax.ppermute(send, axes, swap)
    (result,) = call(output_kernel, [(band, F32)], (mine, other, root), [VMEM, VMEM, HBM], [pltpu.SemaphoreType.DMA])
    return result.reshape(1, channels, rows, lon)


def solution(mesh):
    in_specs = (P("tm", None, "lat", None), P("tm", None, "lat", None), P("tm")) + (P(),) * 7
    out_specs = P("tm", None, "lat", None)

    return jax.shard_map(shards, mesh=mesh, in_specs=in_specs, out_specs=out_specs, check_vma=False)
```

```python
import functools
import math

import jax
import jax.numpy as jnp
from jax import lax
from jax.experimental import pallas as pl
from jax.experimental.pallas import tpu as pltpu
from jax.sharding import PartitionSpec as P


ITERS = 2
LEVELS = 1000
LANES = 128
LEAD = 8
RADIX = 4
TILE = 24
BF16 = jnp.bfloat16
F32 = jnp.float32
VMEM = pl.BlockSpec(memory_space=pltpu.VMEM)
SMEM = pl.BlockSpec(memory_space=pltpu.SMEM)
HBM = pl.BlockSpec(memory_space=pltpu.HBM)
VMEM_OR_HBM = pl.BlockSpec(memory_space=pl.ANY)
PAD = 88
LIMIT = pltpu.CompilerParams(vmem_limit_bytes=24 << 20)


def place():
    t, l = lax.axis_index("tm"), lax.axis_index("lat")
    return t, l, t % 2, (t + l) % 2


def level_of(index):
    return 2.0 * jnp.exp(index * (math.log(0.1) / (LEVELS - 1)))


def prep_kernel(idx_ref, traj_hbm, own_ref, inner_ref, swap_ref, side_ref, traj_ref, v_ref, sem):
    channels, rows, _, lon = traj_ref.shape
    half = rows // 2
    _, _, _, h = place()
    copy = pltpu.make_async_copy(traj_hbm, traj_ref, sem)
    copy.start()
    v_ref[channels:, :] = jnp.ones((PAD - channels, rows * lon), BF16)
    copy.wait()
    for r in range(rows):
        v_ref[:channels, r * lon : (r + 1) * lon] = traj_ref[:, r, 0, :].astype(BF16)
    span, near = (half + 2) * lon, 2 * lon

    def cut(upper):
        low, high = v_ref[:, :span], v_ref[:, lon : lon + span]
        first, last = v_ref[:, :near], v_ref[:, (rows - 2) * lon :]
        own_ref[...] = v_ref[:, : half * lon] if upper else v_ref[:, half * lon :]
        inner_ref[...] = v_ref[:, half * lon : span] if upper else v_ref[:, lon : half * lon]
        swap_ref[...] = high if upper else low
        side_ref[...] = first if upper else last

    @pl.when(h == 0)
    def _():
        cut(True)

    @pl.when(h == 1)
    def _():
        cut(False)

    index = idx_ref[0]
    swap_ref[PAD - 2 : PAD - 1, :] = jnp.full((1, span), index // 32, F32).astype(BF16)
    swap_ref[PAD - 1 : PAD, :] = jnp.full((1, span), index % 32, F32).astype(BF16)


def condition_of(index, time_weight):
    half_width = index.shape[1]
    level = level_of(index)
    step = lax.broadcasted_iota(jnp.int32, index.shape, 1).astype(F32)
    angle = jnp.log(level) * jnp.exp(step * (-math.log(100.0) / half_width))
    features = jnp.concatenate([jnp.cos(angle), jnp.sin(angle)], axis=1)
    z = jnp.dot(features, time_weight, precision=lax.Precision.HIGHEST, preferred_element_type=F32)
    return z / (1.0 + jnp.exp(-z)), level


def fill_embedding(all_ref, emb, cond):
    channels, width = emb.shape
    all_ref[:channels, :] = emb
    all_ref[channels:, :] = jnp.zeros((PAD - channels, width), BF16)
    rest = cond
    for k in range(3):
        piece = rest.astype(BF16)
        all_ref[channels + k : channels + k + 1, :] = piece
        rest = rest - piece.astype(F32)


def embed_row(turned, r, lon, emb_all):
    return jnp.dot(turned[r * lon : (r + 1) * lon, :], emb_all, preferred_element_type=F32).astype(BF16)


def store_row(act_ref, row, a, lon):
    a = a.astype(F32)
    for c in range(a.shape[1] // LANES):
        piece = a[:, c * LANES : (c + 1) * LANES]
        act_ref[c, row, LEAD : LEAD + lon, :] = piece
        act_ref[c, row, 0:LEAD, :] = piece[lon - LEAD : lon, :]
        act_ref[c, row, LEAD + lon : 2 * LEAD + lon, :] = piece[0:LEAD, :]


def conv_tile(act_ref, dw_ref, c, col, tile, half, rows, shift, sums):
    taps = {}
    for rr in rows:
        for j in range(5):
            at = LEAD - 2 + j + col
            x = act_ref[c, rr - shift, at : at + tile, :]
            for o in range(half):
                q = (rr - o) * 5 + j
                if 0 <= rr - o < 5:
                    if q not in taps:
                        taps[q] = dw_ref[q : q + 1, c * LANES : (c + 1) * LANES]
                    v = x * taps[q]
                    sums[o] = v if sums[o] is None else sums[o] + v
    return sums


def near_body(states, emb_alls, dw_ref, act_refs, keep_ref, partial_ref, half, lon):
    for slot, (state, emb_all, act_ref) in enumerate(zip(states, emb_alls, act_refs)):
        chunks = emb_all.shape[1] // LANES
        turned = state[...].T
        for r in range(half):
            a = embed_row(turned, r, lon, emb_all[...])
            keep_ref[slot, r * lon : (r + 1) * lon, :] = a
            store_row(act_ref, r, a, lon)
    for slot, act_ref in enumerate(act_refs):
        for c in range(chunks):
            for k in range(lon // TILE):
                rows = range(2, 2 + half)
                sums = conv_tile(act_ref, dw_ref, c, k * TILE, TILE, half, rows, 2, [None] * half)
                for o in range(half):
                    partial_ref[slot, c, o, k * TILE : (k + 1) * TILE, :] = sums[o]


def near_first_kernel(
    half, idx_ref, own_ref, emb_ref, dw_ref, time_hbm, noise_hbm, traj_hbm,
    emb_all, coef_ref, keep_ref, partial_ref, g_own, g_send,
    act_ref, time_ref, noise_ref, traj_ref, sems,
):
    _, rows, _, lon = noise_ref.shape
    t, _, _, h = place()
    time_c = pltpu.make_async_copy(time_hbm, time_ref, sems.at[0])
    noise_c = pltpu.make_async_copy(noise_hbm, noise_ref, sems.at[1])
    time_c.start()
    noise_c.start()
    index = jnp.full((8, time_ref.shape[0] // 2), idx_ref[0], F32)
    time_c.wait()
    cond, level = condition_of(index, time_ref[...])
    coef_ref[...] = 0.125 * level[:, :LANES]
    fill_embedding(emb_all, emb_ref[...], cond[0:1, :])
    near_body((own_ref,), (emb_all,), dw_ref, (act_ref,), keep_ref, partial_ref, half, lon)
    noise_c.wait()
    scale = 0.125 * jnp.sqrt(level_of(jnp.full((1, lon), idx_ref[0], F32)))

    def emit(upper, anchored):
        for r in range(rows):
            value = scale * noise_ref[:, r, 0, :]
            if anchored:
                value = value + traj_ref[:, r, 0, :]
            cols = slice((r % half) * lon, (r % half + 1) * lon)
            target = g_own if (r < half) == upper else g_send
            target[:, cols] = value

    @pl.when(t == 0)
    def _():
        root = pltpu.make_async_copy(traj_hbm, traj_ref, sems.at[2])
        root.start()
        root.wait()

    for upper in (True, False):
        for anchored in (True, False):

            @pl.when((h == (0 if upper else 1)) & ((t == 0) == anchored))
            def _():
                emit(upper, anchored)


def near_later_kernel(half, lon, own_ref, part_ref, emb_own, emb_part, dw_ref, keep_ref, partial_ref, act0, act1):
    near_body((own_ref, part_ref), (emb_own, emb_part), dw_ref, (act0, act1), keep_ref, partial_ref, half, lon)


def spread_out(main, extra):
    done = 0
    for i, unit in enumerate(main):
        unit()
        while done < len(extra) and done * len(main) < (i + 1) * len(extra):
            extra[done]()
            done += 1
    for unit in extra[done:]:
        unit()


def pack(ref, value):
    channels, points = value.shape
    for k in range(PAD // 8):
        piece = value[8 * k : min(8 * k + 8, channels), :]
        ref[: piece.shape[0], k * points : (k + 1) * points] = piece.astype(ref.dtype)


def unpack(ref, channels, points, start=0, count=None):
    count = points if count is None else count
    pieces = []
    for k in range(PAD // 8):
        at = k * points + start
        pieces.append(ref[: min(8, channels - 8 * k), at : at + count].astype(F32))
    return jnp.concatenate(pieces, axis=0)


def packed(points, dtype):
    return ((8, PAD // 8 * points), dtype)


def finish(first_sum, second_sum, known, sent_ref, even_ref, total_ref):
    _, _, y, _ = place()
    even_ref[...] = jnp.where(y == 0, first_sum, second_sum)
    total = first_sum + second_sum
    if known is not None:
        total = total - unpack(known, *total.shape)
    pack(sent_ref, total)
    pack(total_ref, total)


def finish_kernel(inc_own, drift_part, g_part, sent_ref, even_ref, total_ref):
    finish(inc_own[...], drift_part[...] + g_part[...], None, sent_ref, even_ref, total_ref)


def far_kernel(first, sizes, *refs):
    half, lon, chunks, ff, _ = sizes
    width = chunks * LANES
    refs = list(refs)

    def take(n):
        got = refs[:n]
        del refs[:n]
        return got

    if first:
        inner_own, part5, outer = take(3)
        emb_own, coef_own, keep_in, partial, emb_ref, time_hbm = take(6)
    else:
        inner, outer = take(2)
        emb_own, emb_part, coef_own, coef_part, keep_in, partial, sent_in = take(7)
    dw_ref, gain_ref, up_ref, down_ref, out_ref, g_own = take(6)
    if first:
        inc_own, drift_part, emb_part, coef_part = take(4)
    else:
        (g_part,) = take(1)
        sent_ref, even_ref, total_ref = take(3)
    act0, act1, conv_ref, norm_ref, up_out, hid_ref, bo_ref = take(7)
    if first:
        time_ref, time_sem = take(2)

    _, _, _, h = place()
    acts = (act0, act1)
    inside = 5 * (1 - h)
    outside = 5 * h
    near = 2 * lon
    whole = (False, first)
    if first:
        time_c = pltpu.make_async_copy(time_hbm, time_ref, time_sem)
        time_c.start()

    def condition_unit():
        quarter = width // 2
        row = lambda k: part5[PAD - k : PAD - k + 1, :quarter].astype(F32)
        index = jnp.broadcast_to(row(2) * 32.0 + row(1), (8, quarter))
        cond, level = condition_of(index, time_ref[...])
        coef_part[...] = 0.125 * level[:, :LANES]
        fill_embedding(emb_part, emb_ref[...], cond[0:1, :])

    def embed_units(slot):
        emb_all = (emb_own, emb_part)[slot]
        if not first:
            pieces = (
                (inner, slice((1 - slot) * near, (2 - slot) * near), inside),
                (outer, slice(slot * near, (slot + 1) * near), outside),
            )
        elif slot == 0:
            pieces = ((inner_own, slice(0, near), inside), (outer, slice(0, near), outside))
        else:
            pieces = ((part5, slice(0, (half + 2) * lon), 2 * (1 - h)), (outer, slice(near, 2 * near), outside))
        units = []
        for ref, cols, base in pieces:
            held = []

            def unit(r, ref=ref, cols=cols, base=base, held=held):
                if not held:
                    held.append(ref[:, cols].T)
                store_row(acts[slot], base + r, embed_row(held[0], r, lon, emb_all[...]), lon)

            units += [functools.partial(unit, r) for r in range((cols.stop - cols.start) // lon)]
        return units

    part = lon // 2

    def conv_units(b):
        slot, p = b // 2, b % 2
        flip = b % 2
        rows = range(half + 4) if whole[slot] else (0, 1, half + 2, half + 3)

        def tile_unit(c, k):
            col = p * part + k * TILE
            sums = [None if whole[slot] else partial[slot, c, o, col : col + TILE, :] for o in range(half)]
            sums = conv_tile(acts[slot], dw_ref, c, col, TILE, half, rows, 0, sums)
            for o in range(half):
                conv_ref[flip, c, o, k * TILE : (k + 1) * TILE, :] = sums[o]

        def norm_unit(o, k):
            span = slice(k * 48, (k + 1) * 48)
            x = [conv_ref[flip, c, o, span, :] for c in range(chunks)]
            mean = jnp.sum(functools.reduce(jnp.add, x), axis=1, keepdims=True) * (1.0 / width)
            x = [v - mean for v in x]
            var = jnp.sum(functools.reduce(jnp.add, [v * v for v in x]), axis=1, keepdims=True) * (1.0 / width)
            inv = lax.rsqrt(var + 1e-06)
            for c, v in enumerate(x):
                lane = slice(c * LANES, (c + 1) * LANES)
                value = (v * inv * gain_ref[:, lane]).astype(BF16)
                norm_ref[flip, o * part + k * 48 : o * part + (k + 1) * 48, lane] = value

        return [functools.partial(tile_unit, c, k) for c in range(chunks) for k in range(part // TILE)] + [
            functools.partial(norm_unit, o, k) for o in range(half) for k in range(part // 48)
        ]

    k0 = math.sqrt(2.0 / math.pi)

    def mix_units(b):
        slot, p = b // 2, b % 2
        flip = b % 2

        def up_unit(n):
            up_out[n % 2] = jnp.dot(norm_ref[flip], up_ref[:, n * 256 : (n + 1) * 256], preferred_element_type=F32)

        def gelu_unit(n, o):
            u = up_out[n % 2, o * part : (o + 1) * part, :]
            value = (u + u * jnp.tanh(u * (k0 + (k0 * 0.044715) * (u * u)))).astype(BF16)
            hid_ref[flip, o * part : (o + 1) * part, n * 256 : (n + 1) * 256] = value

        def down_unit(m):
            d = jnp.dot(hid_ref[flip], down_ref[:, m * 256 : (m + 1) * 256], preferred_element_type=F32)
            lane = slice(m * 256, (m + 1) * 256)
            for o in range(half):
                span = slice(o * lon + p * part, o * lon + (p + 1) * part)
                if whole[slot]:
                    c = 2 * m
                    at = slice(LEAD + p * part, LEAD + (p + 1) * part)
                    a = jnp.concatenate([acts[slot][c, 2 + o, at, :], acts[slot][c + 1, 2 + o, at, :]], axis=1)
                else:
                    a = keep_in[slot, span, lane].astype(F32)
                bo_ref[slot, span, lane] = (a + 0.5 * d[o * part : (o + 1) * part, :]).astype(BF16)

        steps = ff // 256
        units = [functools.partial(up_unit, 0)]
        for n in range(steps):
            if n + 1 < steps:
                units.append(functools.partial(up_unit, n + 1))
            units += [functools.partial(gelu_unit, n, o) for o in range(half)]
        return units + [functools.partial(down_unit, m) for m in range(width // 256)]

    incs = []

    def out_unit(slot):
        drift = lax.dot_general(out_ref[...], bo_ref[slot], (((1,), (1,)), ((), ())), preferred_element_type=F32)
        drift = (coef_own, coef_part)[slot][0:1, 0:1] * drift
        if slot == 0:
            drift = drift + g_own[...]
        elif not first:
            drift = drift + g_part[...]
        if first:
            (inc_own, drift_part)[slot][...] = drift
        else:
            incs.append(drift)

    for unit in embed_units(0):
        unit()
    if first:
        spread_out(conv_units(0), [])
        time_c.wait()
        condition_unit()
        spread_out(conv_units(1), embed_units(1) + mix_units(0))
    else:
        spread_out(conv_units(0), embed_units(1))
        spread_out(conv_units(1), mix_units(0))
    spread_out(conv_units(2), mix_units(1))
    spread_out(conv_units(3), mix_units(2) + [functools.partial(out_unit, 0)])
    for unit in mix_units(3):
        unit()
    out_unit(1)
    if not first:
        finish(incs[0], incs[1], sent_in, sent_ref, even_ref, total_ref)


def cost(flops, nbytes=1 << 20):
    return pl.CostEstimate(flops=int(flops), bytes_accessed=nbytes, transcendentals=0)


def act_scratch(chunks, rows, lon):
    return pltpu.VMEM((chunks, rows, lon + 2 * LEAD, LANES), F32)


def far(first, head, weights, half, lon):
    _, _, up, _, _, g_own = weights[:6]
    channels, points = g_own.shape
    width, ff = up.shape
    chunks = width // LANES
    block = points // 2
    grid = ((channels, points), F32)
    outs = [grid, grid] if first else [packed(points, BF16), grid, packed(points, F32)]
    specs = [VMEM] * (len(head) + len(weights))
    scratch = [act_scratch(chunks, half + 4, lon)] * 2 + [
        pltpu.VMEM((2, chunks, half, lon // 2, LANES), F32),
        pltpu.VMEM((2, block, width), BF16),
        pltpu.VMEM((2, block, 256), F32),
        pltpu.VMEM((2, block, ff), BF16),
        pltpu.VMEM((2, points, width), BF16),
    ]
    if first:
        outs += [((PAD, width), BF16), ((8, LANES), F32)]
        specs[len(head) - 1] = HBM
        scratch += [pltpu.VMEM(head[-1].shape, F32), pltpu.SemaphoreType.DMA]
    return call(
        functools.partial(far_kernel, first, (half, lon, chunks, ff, channels)),
        outs,
        (*head, *weights),
        specs,
        scratch,
        cost(2 * 2 * points * width * (channels * 2 + 2 * ff + 25)),
    )


def edges_kernel(near, own_ref, part_ref, out_ref):
    _, _, _, h = place()
    out_ref[:, :near] = own_ref[...]

    @pl.when(h == 0)
    def _():
        out_ref[:, near:] = part_ref[:, :near]

    @pl.when(h == 1)
    def _():
        out_ref[:, near:] = part_ref[:, part_ref.shape[1] - near :]


def relay_kernel(total_ref, got_ref, out_ref):
    out_ref[...] = (total_ref[...] + got_ref[...].astype(F32)).astype(BF16)


def middle_kernel(count, chained, lon, *refs):
    gots, refs = refs[:count], list(refs[count:])
    if chained:
        total_ref, offset_ref = refs.pop(0), refs.pop()
        arrived = gots[0][...].astype(F32)
        for g in gots[1:]:
            arrived = arrived + g[...].astype(F32)
        offset_ref[...] = (total_ref[...] + arrived).astype(BF16).astype(F32) - arrived
    even, own3, part5, sum_ref, own_ref, part_ref, inner_ref, outer_ref = refs
    channels, points = even.shape
    t, _, y, h = place()
    near = 2 * lon
    total = unpack(gots[0], channels, points)
    for g in gots[1:]:
        total = total + unpack(g, channels, points)
    sum_ref[...] = total
    odd = (total + even[...]).astype(BF16)
    flat = total.astype(BF16)
    for ref in (own_ref, part_ref, inner_ref, outer_ref):
        ref[channels:, :] = jnp.ones((PAD - channels, ref.shape[1]), BF16)

    def emit(parity, upper):
        shift = 0 if upper else near
        start = own3[:channels, :] if parity == 0 else part5[:channels, shift : shift + points]
        state = jnp.where(t < 2, start.astype(F32), flat.astype(F32)).astype(BF16)
        pair = (state, odd) if parity == 0 else (odd, state)
        own_ref[:channels, :] = pair[0]
        part_ref[:channels, :] = pair[1]
        for k, s in enumerate(pair):
            cols = slice(k * near, (k + 1) * near)
            low, high = s[:, :near], s[:, points - near :]
            inner_ref[:channels, cols] = high if upper else low
            outer_ref[:channels, cols] = low if upper else high

    for parity in range(2):
        for half_at in range(2):

            @pl.when((y == parity) & (h == half_at))
            def _():
                emit(parity, half_at == 0)


def ending_kernel(count, *refs):
    gots, (before, even, mine_ref, send_ref) = refs[:count], refs[count:]
    _, _, y, _ = place()
    total = before[...]
    for g in gots:
        total = total + unpack(g, *total.shape)
    odd = total + even[...]
    mine_ref[...] = jnp.where(y == 0, total, odd)
    pack(send_ref, jnp.where(y == 0, odd, total))


def output_kernel(mine, other, traj_hbm, out_ref, sem):
    channels, rows, _, lon = out_ref.shape
    half = rows // 2
    t, _, _, h = place()

    def emit(upper):
        for r in range(rows):
            start = (r % half) * lon
            if (r < half) == upper:
                out_ref[:, r, 0, :] = mine[:, start : start + lon]
            else:
                out_ref[:, r, 0, :] = unpack(other, channels, half * lon, start, lon)

    @pl.when((h == 0) & (t > 0))
    def _():
        emit(True)

    @pl.when((h == 1) & (t > 0))
    def _():
        emit(False)

    @pl.when(t == 0)
    def _():
        copy = pltpu.make_async_copy(traj_hbm, out_ref, sem)
        copy.start()
        copy.wait()


def call(body, outs, ins, specs=None, scratch=(), estimate=None):
    return pl.pallas_call(
        body,
        out_shape=tuple(jax.ShapeDtypeStruct(s, d) for s, d in outs),
        in_specs=specs or [VMEM] * len(ins),
        out_specs=tuple([VMEM] * len(outs)),
        scratch_shapes=list(scratch),
        compiler_params=LIMIT,
        cost_estimate=estimate,
    )(*ins)


def chain(sent, total, groups):
    gots = []
    for last in range(groups - 1):
        if last:
            (sent,) = call(relay_kernel, [(total.shape, BF16)], (total, gots[-1]))
        gots.append(lax.ppermute(sent, "tm", [(2 * last + y, 2 * last + 2 + y) for y in range(2)]))
    return gots


def exchange(sent, total, groups, memory):
    gots, kept = [], []
    base, moved, unit = sent, None, 1
    while unit < groups:
        if unit > 1:
            rest = memory[len(kept)] if memory else 0.0
            sent = (total + moved + rest).astype(BF16)
            kept.append(base.astype(F32) + moved + rest - sent.astype(F32))
        for step in range(1, RADIX):
            shift = 2 * step * unit
            if shift < 2 * groups:
                gots.append(lax.ppermute(sent, "tm", [(i, i + shift) for i in range(2 * groups - shift)]))
        unit *= RADIX
        if groups > RADIX:
            moved = functools.reduce(jnp.add, [g.astype(F32) for g in gots])
    return gots, kept


def shards(
    traj, noise, step_index, embed_weight, time_weight, dw_weight, ln_gain, up_weight, down_weight, out_weight,
):
    times, bands = lax.axis_size("tm"), lax.axis_size("lat")
    groups = times // 2
    channels, rows, lon = traj.shape[1:]
    half = rows // 2
    width = embed_weight.shape[1]
    points, span, near = half * lon, (half + 2) * lon, 2 * lon
    axes = ("tm", "lat")

    def at(a, b):
        return a * bands + b

    cells = [(a, b, (a + b) % 2) for a in range(times) for b in range(bands)]
    swap = [(at(a, b), at(a ^ 1, b)) for a, b, _ in cells]
    side = [(at(a, b), at(a, b + (1 if c else -1))) for a, b, c in cells if 0 <= b + (1 if c else -1) < bands]

    root = traj.reshape(channels, rows, 1, lon)
    draws = noise.reshape(channels, rows, 1, lon)
    band = (channels, rows, 1, lon)
    chunks = width // LANES
    own3, inner_own, to_swap, to_side = call(
        prep_kernel,
        [((PAD, points), BF16), ((PAD, near), BF16), ((PAD, span), BF16), ((PAD, near), BF16)],
        (step_index, root),
        [SMEM, HBM],
        [pltpu.VMEM(band, F32), pltpu.VMEM((PAD, rows * lon), BF16), pltpu.SemaphoreType.DMA],
        cost(1e9),
    )
    part5 = lax.ppermute(to_swap, axes, swap)
    dw = dw_weight.T
    work = 2 * points * width * (2 * channels + 25)

    def kept(slots):
        return [((slots, points, width), BF16), ((slots, chunks, half, lon, LANES), F32)]

    emb_own, coef_own, keep, partial, g_own, g_send = call(
        functools.partial(near_first_kernel, half),
        [((PAD, width), BF16), ((8, LANES), F32)] + kept(1) + [((channels, points), F32)] * 2,
        (step_index, own3, embed_weight, dw, time_weight, draws, root),
        [SMEM, VMEM, VMEM, VMEM, HBM, HBM, HBM],
        [
            act_scratch(chunks, half, lon),
            pltpu.VMEM(time_weight.shape, F32),
            pltpu.VMEM(band, F32),
            pltpu.VMEM(band, F32),
            pltpu.SemaphoreType.DMA((3,)),
        ],
        cost(20 * work),
    )
    (to_side,) = call(functools.partial(edges_kernel, near), [((PAD, 2 * near), BF16)], (to_side, part5))
    outer = lax.ppermute(to_side, axes, side)
    g_part = lax.ppermute(g_send, axes, swap)
    weights = (dw, ln_gain.reshape(1, width), up_weight, down_weight, out_weight.T, g_own)
    staged = groups > RADIX
    inc_own, drift_part, emb_part, coef_part = far(
        True,
        (inner_own, part5, outer, emb_own, coef_own, keep, partial, embed_weight, time_weight),
        weights,
        half,
        lon,
    )
    sums = [packed(points, BF16), ((channels, points), F32), packed(points, F32)]
    sent, even, total = call(finish_kernel, sums, (inc_own, drift_part, g_part))

    def collect(sent, total, memory):
        if staged:
            return exchange(sent, total, groups, memory)
        return chain(sent, total, groups), memory

    gots, memory = collect(sent, total, None)
    before = None
    for _ in range(1, ITERS):
        before, s_own, s_part, inner, outer, *offset = call(
            functools.partial(middle_kernel, len(gots), not staged, lon),
            [((channels, points), F32)]
            + [((PAD, points), BF16)] * 2
            + [((PAD, 2 * near), BF16)] * 2
            + [packed(points, F32)] * (not staged),
            (*gots, *([] if staged else [total]), even, own3, part5),
        )
        known = sent.astype(F32) if staged else offset[0]
        inner = lax.ppermute(inner, axes, swap)
        outer = lax.ppermute(outer, axes, side)
        keep, partial = call(
            functools.partial(near_later_kernel, half, lon),
            kept(2),
            (s_own, s_part, emb_own, emb_part, dw),
            scratch=[act_scratch(chunks, half, lon)] * 2,
            estimate=cost(20 * work),
        )
        sent, even, total = far(
            False,
            (inner, outer, emb_own, emb_part, coef_own, coef_part, keep, partial, known),
            weights + (g_part,),
            half,
            lon,
        )
        gots, memory = collect(sent, total, memory)
    mine, send = call(
        functools.partial(ending_kernel, len(gots)),
        [((channels, points), F32), packed(points, F32)],
        (*gots, before, even),
    )
    other = lax.ppermute(send, axes, swap)
    (result,) = call(output_kernel, [(band, F32)], (mine, other, root), [VMEM, VMEM, HBM], [pltpu.SemaphoreType.DMA])
    return result.reshape(1, channels, rows, lon)


def solution(mesh):
    in_specs = (P("tm", None, "lat", None), P("tm", None, "lat", None), P("tm")) + (P(),) * 7
    out_specs = P("tm", None, "lat", None)

    return jax.shard_map(shards, mesh=mesh, in_specs=in_specs, out_specs=out_specs, check_vma=False)
```
